32 devices in a mesh: seq: 16 (over z, y, x), head: 2 (over core).
Axes of the slice: x: 2, y: 2, z: 4, core: 2. Of those that a mesh axis runs over, the one named last changes fastest.
Arguments:
- query_act: bfloat16 [8192, 4096], P('seq', 'head'), may hold values from -6 to 6
- key_act: bfloat16 [8192, 4096], P('seq', 'head'), may hold values from -6 to 6
- value_act: bfloat16 [8192, 4096], P('seq', 'head'), may hold values from -16 to 16
- upstream: bfloat16 [8192, 4096], P('seq', 'head'), may hold values from -6 to 6
- norm_gain: float32 [4096], P('head'), may hold values from 0.1 to 1.9
Outputs:
- grad_query: bfloat16 [8192, 4096], P('seq', 'head')
- grad_key: bfloat16 [8192, 4096], P('seq', 'head')
- grad_value: bfloat16 [8192, 4096], P('seq', 'head')
The draws below stay inside these ranges and needn't reach their ends.
All inputs are finite; a program needn't handle non-finite values.
Results may differ from the reference program's by a relative error of at most 0.0058.
Values sent between devices are 32-bit elements; how exact they have to be, the bound alone decides.
No kernel may reach another device: no remote copies, remote signals or barrier semaphores. Data moves between devices by JAX's collectives and lax.ppermute only.
A program may use at most 128 MiB of HBM per device.

```python
import jax
import jax.numpy as jnp
from jax import lax

HEADS = 32
HD = 128
CH = 128
SEQ = 8192
FEATURES = 4096


def draw_value_act(key, part):
    head_index = jnp.arange(HEADS * HD) // HD
    position = head_index.astype(jnp.float32) / max(HEADS - 1, 1)
    factor = 3.0 ** position
    sample = jax.random.normal(key, (SEQ, HEADS * HD), jnp.float32)
    return jnp.clip(sample * factor[None, :], -16.0, 16.0).astype(jnp.bfloat16)


def shard_levels(key, dims, cuts, low, largest):
    gain, own = 1.0, jax.random.fold_in(key, 6)
    for axis_at, shards_of in cuts:
        draws = jnp.exp(jax.random.uniform(jax.random.fold_in(own, axis_at), (shards_of,), jnp.float32, low / len(cuts), largest / len(cuts)))
        gain = gain * jnp.repeat(draws, dims[axis_at] // shards_of).reshape([-1 if axis == axis_at else 1 for axis in range(len(dims))])
    return gain


def bell_draw(stream_key, extent, scale, reach, cuts=(), held_as=jnp.bfloat16):
    entries = jax.random.normal(stream_key, extent, jnp.float32) * scale
    if len(cuts) > 0:
        entries = shard_levels(stream_key, extent, cuts, -0.22, 0.18) * entries
    return jnp.clip(entries, min=-reach, max=reach).astype(held_as)


def setup_inputs(seed: int = 0) -> dict:
    keys = jax.random.split(jax.random.key(seed), 6)
    return {
        "query_act": bell_draw(keys[0], (SEQ, FEATURES), 1.0, 6.0, ((0, 16), (1, 2))),
        "key_act": bell_draw(keys[1], (SEQ, FEATURES), 1.0, 6.0, ((0, 16), (1, 2))),
        "value_act": draw_value_act(jax.random.fold_in(keys[5], 71), 0),
        "upstream": bell_draw(keys[3], (SEQ, FEATURES), 1.0, 6.0, ((0, 16), (1, 2))),
        "norm_gain": jnp.clip(1.0 + 0.18 * jax.random.normal(keys[4], (FEATURES,), jnp.float32), 0.1, 1.9),
    }


def causal_mask():
    rows = lax.broadcasted_iota(jnp.int32, (CH, CH), 0)
    columns = lax.broadcasted_iota(jnp.int32, (CH, CH), 1)
    return (columns <= rows).astype(jnp.float32)

def rounded(values):
    return lax.optimization_barrier(values.astype(jnp.bfloat16)).astype(jnp.float32)

def exclusive_prefix(states):
    zeros = jnp.zeros_like(states[:1])
    return jnp.concatenate([zeros, jnp.cumsum(states, 0)[:-1]], 0)

def exclusive_suffix(states):
    after = jnp.cumsum(states[::-1], 0)[::-1]
    return jnp.concatenate([after[1:], jnp.zeros_like(states[:1])], 0)

def split_heads(matrix):
    return matrix.reshape(SEQ // CH, CH, HEADS, HD).transpose(2, 0, 1, 3)

def join_heads(blocks):
    return blocks.transpose(1, 2, 0, 3).reshape(SEQ, HEADS * HD)

def head_forward(operands):
    query_blk = operands[0].astype(jnp.float32)
    key_blk = operands[1].astype(jnp.float32)
    value_blk = operands[2].astype(jnp.float32)
    kv_state = rounded(exclusive_prefix(jnp.einsum('cti,ctj->cij', key_blk, value_blk)))
    fwd_scores = rounded(jnp.einsum('cti,csi->cts', query_blk, key_blk) * causal_mask())
    return jnp.einsum('cts,csj->ctj', fwd_scores, value_blk) + jnp.einsum('cti,cij->ctj', query_blk, kv_state)

def head_backward(operands):
    query_blk = operands[0].astype(jnp.float32)
    key_blk = operands[1].astype(jnp.float32)
    value_blk = operands[2].astype(jnp.float32)
    grad_blk = operands[3].astype(jnp.float32)
    causal = causal_mask()
    kv_state = rounded(exclusive_prefix(jnp.einsum('cti,ctj->cij', key_blk, value_blk)))
    fwd_scores = rounded(jnp.einsum('cti,csi->cts', query_blk, key_blk) * causal)
    back_scores = rounded(jnp.einsum('ctj,csj->cts', grad_blk, value_blk) * causal)
    qd_state = rounded(exclusive_suffix(jnp.einsum('cti,ctj->cij', query_blk, grad_blk)))
    grad_q = jnp.einsum('cts,csi->cti', back_scores, key_blk) + jnp.einsum('ctj,cij->cti', grad_blk, kv_state)
    grad_k = jnp.einsum('cts,cti->csi', back_scores, query_blk) + jnp.einsum('csj,cij->csi', value_blk, qd_state)
    grad_v = jnp.einsum('cts,ctj->csj', fwd_scores, grad_blk) + jnp.einsum('csi,cij->csj', key_blk, qd_state)
    return (grad_q.astype(jnp.bfloat16), grad_k.astype(jnp.bfloat16), grad_v.astype(jnp.bfloat16))

def reference(query_act, key_act, value_act, upstream, norm_gain):
    query_heads = split_heads(query_act)
    key_heads = split_heads(key_act)
    value_heads = split_heads(value_act)
    attention = lax.map(head_forward, (query_heads, key_heads, value_heads))
    guided = norm_gain.reshape(HEADS, 1, 1, HD) * split_heads(upstream).astype(jnp.float32)
    inverse = lax.rsqrt(lax.optimization_barrier(jnp.mean(attention * attention, axis=(0, 3))) + 1e-06)[None, :, :, None]
    cross = lax.optimization_barrier(jnp.mean(guided * attention, axis=(0, 3)))[None, :, :, None]
    grad_attn = lax.optimization_barrier((inverse * guided - inverse ** 3 * cross * attention).astype(jnp.bfloat16))
    grad_q, grad_k, grad_v = lax.map(head_backward, (query_heads, key_heads, value_heads, grad_attn))
    return (join_heads(grad_q), join_heads(grad_k), join_heads(grad_v))
```

```python
import jax
import jax.numpy as jnp
from jax import lax
from jax.sharding import PartitionSpec as P

HEADS = 32
HD = 128
CH = 128


def group_size(peers, heads):
    size = 1
    while size < 8 and peers % (2 * size) == 0 and heads % (2 * size) == 0:
        size *= 2
    return size


def partners(peers, j):
    return [(s, s ^ j) for s in range(peers)]


def shifted(peers, by, reverse):
    pairs = [(s, s + by) for s in range(peers - by)]
    return [(b, a) for a, b in pairs] if reverse else pairs


def exclusive(total, axis, reverse):
    peers, position = lax.axis_size(axis), lax.axis_index(axis)
    group = group_size(peers, total.shape[0])
    heads = total.shape[0] // group
    spot = position % group
    sent = [
        lax.dynamic_slice_in_dim(total, (spot ^ j) * heads, heads, 0) for j in range(group)
    ]
    got = [sent[0]] + [lax.ppermute(sent[j], axis, partners(peers, j)) for j in range(1, group)]
    count = peers // group
    carry = jnp.zeros_like(got[0])
    if count > 1:
        carry = lax.ppermute(sum(got), axis, shifted(peers, group, reverse))
        step = 1
        while step < count - 1:
            carry = carry + lax.ppermute(carry, axis, shifted(peers, group * step, reverse))
            step *= 2
    back = []
    for j in range(group):
        part = carry
        for i in range(group):
            inside = (spot ^ i) > (spot ^ j) if reverse else (spot ^ i) < (spot ^ j)
            part = part + jnp.where(inside, got[i], 0.0)
        back.append(part if j == 0 else lax.ppermute(part, axis, partners(peers, j)))
    pieces = jnp.stack(back)
    order = jnp.arange(group) ^ spot
    return pieces[order].reshape(total.shape)


def causal_mask():
    rows = lax.broadcasted_iota(jnp.int32, (CH, CH), 0)
    columns = lax.broadcasted_iota(jnp.int32, (CH, CH), 1)
    return (columns <= rows).astype(jnp.float32)


def block_table(count, before):
    rows = lax.broadcasted_iota(jnp.int32, (count, count), 0)
    columns = lax.broadcasted_iota(jnp.int32, (count, count), 1)
    if before:
        return (columns < rows).astype(jnp.float32)
    return (columns > rows).astype(jnp.float32)


def local_prefix(states):
    table = block_table(states.shape[0], True)
    return jnp.einsum(
        "dc,chij->dhij",
        table,
        states,
        precision=lax.Precision.HIGHEST,
        preferred_element_type=jnp.float32,
    )


def local_suffix(states):
    table = block_table(states.shape[0], False)
    return jnp.einsum(
        "dc,chij->dhij",
        table,
        states,
        precision=lax.Precision.HIGHEST,
        preferred_element_type=jnp.float32,
    )


def on_device(query_act, key_act, value_act, upstream, norm_gain):
    rows_dev = query_act.shape[0]
    heads_dev = query_act.shape[1] // HD
    groups = rows_dev // CH
    block_shape = (groups, CH, heads_dev, HD)
    query_blk = query_act.reshape(block_shape)
    key_blk = key_act.reshape(block_shape)
    value_blk = value_act.reshape(block_shape)
    causal = causal_mask()[None, None]
    kv_group = jnp.einsum("cthi,cthj->chij", key_blk, value_blk, preferred_element_type=jnp.float32)
    kv_total = jnp.sum(kv_group, 0)
    kv_before = exclusive(kv_total, "seq", False)
    kv_state = (kv_before[None] + local_prefix(kv_group)).astype(jnp.bfloat16)
    fwd_scores = (
        jnp.einsum("cthi,cshi->chts", query_blk, key_blk, preferred_element_type=jnp.float32)
        * causal
    ).astype(jnp.bfloat16)
    attention = jnp.einsum(
        "chts,cshj->cthj", fwd_scores, value_blk, preferred_element_type=jnp.float32
    )
    attention = attention + jnp.einsum(
        "cthi,chij->cthj", query_blk, kv_state, preferred_element_type=jnp.float32
    )
    guided = norm_gain.reshape(heads_dev, HD) * upstream.reshape(block_shape).astype(jnp.float32)
    squares, crossed = lax.psum(
        (jnp.sum(attention * attention, (2, 3)), jnp.sum(guided * attention, (2, 3))), "head"
    )
    total_width = HEADS * HD
    inverse = lax.rsqrt(squares / total_width + 1e-06)[:, :, None, None]
    cross_mean = (crossed / total_width)[:, :, None, None]
    grad_attn = (inverse * guided - inverse**3 * cross_mean * attention).astype(jnp.bfloat16)
    back_scores = (
        jnp.einsum("cthj,cshj->chts", grad_attn, value_blk, preferred_element_type=jnp.float32)
        * causal
    ).astype(jnp.bfloat16)
    qd_group = jnp.einsum(
        "cthi,cthj->chij", query_blk, grad_attn, preferred_element_type=jnp.float32
    )
    qd_own = jnp.sum(qd_group, 0)
    qd_after = exclusive(qd_own, "seq", True)
    qd_state = (qd_after[None] + local_suffix(qd_group)).astype(jnp.bfloat16)
    grad_q = jnp.einsum("chts,cshi->cthi", back_scores, key_blk, preferred_element_type=jnp.float32)
    grad_q = grad_q + jnp.einsum(
        "cthj,chij->cthi", grad_attn, kv_state, preferred_element_type=jnp.float32
    )
    grad_k = jnp.einsum(
        "chts,cthi->cshi", back_scores, query_blk, preferred_element_type=jnp.float32
    )
    grad_k = grad_k + jnp.einsum(
        "cshj,chij->cshi", value_blk, qd_state, preferred_element_type=jnp.float32
    )
    grad_v = jnp.einsum(
        "chts,cthj->cshj", fwd_scores, grad_attn, preferred_element_type=jnp.float32
    )
    grad_v = grad_v + jnp.einsum(
        "cshi,chij->cshj", key_blk, qd_state, preferred_element_type=jnp.float32
    )
    out_shape = (rows_dev, heads_dev * HD)
    return (
        grad_q.astype(jnp.bfloat16).reshape(out_shape),
        grad_k.astype(jnp.bfloat16).reshape(out_shape),
        grad_v.astype(jnp.bfloat16).reshape(out_shape),
    )


def solution(mesh):
    in_specs = (P("seq", "head"), P("seq", "head"), P("seq", "head"), P("seq", "head"), P("head"))
    out_specs = (P("seq", "head"), P("seq", "head"), P("seq", "head"))
    return jax.shard_map(
        on_device, mesh=mesh, in_specs=in_specs, out_specs=out_specs, check_vma=False
    )
```

```python
import functools

import jax
import jax.numpy as jnp
from jax import lax
from jax.experimental import pallas as pl
from jax.experimental.pallas import tpu as pltpu
from jax.sharding import PartitionSpec as P

HD = 128
CH = 128
F32 = jnp.float32
BF16 = jnp.bfloat16


def group_size(peers, heads):
    size = 1
    while size < 8 and peers % (2 * size) == 0 and heads % (2 * size) == 0:
        size *= 2
    return size


def dot(a, b, a_dim, b_dim):
    return lax.dot_general(a, b, (((a_dim,), (b_dim,)), ((), ())), preferred_element_type=F32)


def head_columns(i):
    return slice(i * HD, (i + 1) * HD)


def causal():
    rows = lax.broadcasted_iota(jnp.int32, (CH, CH), 0)
    columns = lax.broadcasted_iota(jnp.int32, (CH, CH), 1)
    return columns <= rows


def store_piece(j, outs, i, value):
    for n, out in enumerate(outs):

        @pl.when(j == n)
        def _():
            out[i] = value


def load_diagonal(j, pieces, wide):
    @pl.when(j == 0)
    def _():
        wide[...] = jnp.zeros_like(wide)

    for n, piece in enumerate(pieces):

        @pl.when(j == n)
        def _():
            for i in range(piece.shape[0]):
                wide[head_columns(i), head_columns(i)] = piece[i].astype(BF16)


def kv_kernel(spot, k_ref, v_ref, *outs):
    j = pl.program_id(0)
    for i in range(outs[0].shape[0]):
        c = head_columns(i)
        store_piece(j, outs, i, dot(k_ref[:, c], v_ref[:, c], 0, 0))


def local_kernel(q_ref, k_ref, v_ref, attn_ref, scores_ref, state_ref):
    rows, width = q_ref.shape
    mask = causal()
    for i in range(width // HD):
        c = head_columns(i)
        state = jnp.zeros((HD, HD), F32)
        for b in range(rows // CH):
            r = slice(b * CH, (b + 1) * CH)
            q, k, v = q_ref[r, c], k_ref[r, c], v_ref[r, c]
            scores = jnp.where(mask, dot(q, k, 1, 1), 0.0).astype(BF16)
            scores_ref[r, c] = scores
            near = state.astype(BF16)
            state_ref[r, c] = near
            attn = dot(scores, v, 1, 0)
            if b:
                attn = attn + dot(q, near, 1, 0)
            attn_ref[r, c] = attn
            if b + 1 < rows // CH:
                state = state + dot(k, v, 0, 0)


def owner_kernel(reverse, spot, *refs):
    count = (len(refs) - 1) // 2
    carry, got, outs = refs[0], refs[1 : 1 + count], refs[1 + count :]
    me = spot[0]
    for n in range(count):
        part = carry[...]
        for m in range(count):
            inside = (me ^ m) > (me ^ n) if reverse else (me ^ m) < (me ^ n)
            if m != n:
                part = part + jnp.where(inside, got[m][...], 0.0)
        outs[n][...] = part


def norm_kernel(count, spot, q_ref, local_ref, u_ref, gain_ref, *refs):
    pieces, (attn_ref, sums_ref, far_ref, wide) = refs[:count], refs[count:]
    j = pl.program_id(0)
    load_diagonal(j, pieces, wide)
    rows, width = q_ref.shape
    attn = local_ref[...] + dot(q_ref[...], wide[...], 1, 0)
    attn_ref[...] = attn
    guided = gain_ref[...] * u_ref[...].astype(F32)
    squares, crossed = attn * attn, guided * attn
    total_sq = squares[:, :HD]
    total_cr = crossed[:, :HD]
    for i in range(1, width // HD):
        total_sq = total_sq + squares[:, head_columns(i)]
        total_cr = total_cr + crossed[:, head_columns(i)]

    @pl.when(j == 0)
    def _():
        sums_ref[:rows] = total_sq
        sums_ref[rows:] = total_cr

    @pl.when(j > 0)
    def _():
        sums_ref[:rows] += total_sq
        sums_ref[rows:] += total_cr

    for i in range(width // HD):
        far_ref[i] = wide[head_columns(i), head_columns(i)]


def grad_kernel(sums_count, features, spot, q_ref, attn_ref, u_ref, gain_ref, *refs):
    sums, (g_ref, *outs), (a_ref, b_ref) = refs[:sums_count], refs[sums_count:-2], refs[-2:]
    j = pl.program_id(0)
    rows, width = q_ref.shape

    @pl.when(j == 0)
    def _():
        total = sums[0][...]
        for other in sums[1:]:
            total = total + other[...]
        mean = jnp.sum(total, axis=1, keepdims=True) / features
        inverse = lax.rsqrt(mean[:rows] + 1e-06)
        a_ref[...] = jnp.broadcast_to(inverse, a_ref.shape)
        b_ref[...] = jnp.broadcast_to(inverse * inverse * inverse * mean[rows:], b_ref.shape)

    for i in range(width // HD):
        c = head_columns(i)
        guided = gain_ref[:, c] * u_ref[:, c].astype(F32)
        grad = (a_ref[...] * guided - b_ref[...] * attn_ref[:, c]).astype(BF16)
        g_ref[:, c] = grad
        store_piece(j, outs, i, dot(q_ref[:, c], grad, 0, 0))


def back_kernel(q_ref, k_ref, v_ref, g_ref, scores_ref, state_ref, far_ref, gq_ref, gk_ref, gv_ref):
    rows, width = q_ref.shape
    mask = causal()
    last = rows // CH - 1
    for i in range(width // HD):
        c = head_columns(i)
        far = far_ref[i].astype(F32)
        state = jnp.zeros((HD, HD), F32)
        for b in range(last, -1, -1):
            r = slice(b * CH, (b + 1) * CH)
            q, k, v, g = q_ref[r, c], k_ref[r, c], v_ref[r, c], g_ref[r, c]
            scores = jnp.where(mask, dot(g, v, 1, 1), 0.0).astype(BF16)
            before = (far + state_ref[r, c].astype(F32)).astype(BF16)
            gq_ref[r, c] = (dot(scores, k, 1, 0) + dot(g, before, 1, 1)).astype(BF16)
            gk = dot(scores, q, 0, 0)
            gv = dot(scores_ref[r, c], g, 0, 0)
            if b < last:
                near = state.astype(BF16)
                gk = gk + dot(v, near, 1, 1)
                gv = gv + dot(k, near, 1, 0)
            gk_ref[r, c] = gk
            gv_ref[r, c] = gv
            if b:
                state = state + dot(q, g, 0, 0)


def finish_kernel(count, spot, k_ref, v_ref, gk_ref, gv_ref, *refs):
    pieces, (gk_out, gv_out, wide) = refs[:count], refs[count:]
    load_diagonal(pl.program_id(0), pieces, wide)
    gk_out[...] = (gk_ref[...] + dot(v_ref[...], wide[...], 1, 1)).astype(BF16)
    gv_out[...] = (gv_ref[...] + dot(k_ref[...], wide[...], 1, 0)).astype(BF16)


def call(kernel, grid, in_specs, out_specs, out_shape, scratch, scalars, args, flops):
    moved = sum(a.size * a.dtype.itemsize for a in args)
    moved += sum(s.size * s.dtype.itemsize for s in out_shape)
    return pl.pallas_call(
        kernel,
        out_shape=out_shape,
        grid_spec=pltpu.PrefetchScalarGridSpec(
            num_scalar_prefetch=len(scalars),
            grid=grid,
            in_specs=in_specs,
            out_specs=out_specs,
            scratch_shapes=scratch,
        ),
        cost_estimate=pl.CostEstimate(flops=flops, bytes_accessed=moved, transcendentals=0),
    )(*scalars, *args)


def on_device(query_act, key_act, value_act, upstream, norm_gain):
    peers, sides = lax.axis_size("seq"), lax.axis_size("head")
    rows, columns = query_act.shape
    heads = columns // HD
    group = group_size(peers, heads)
    owned = heads // group
    width = owned * HD
    spot = jnp.reshape(lax.axis_index("seq") % group, (1,)).astype(jnp.int32)
    gain = norm_gain.reshape(1, columns)
    shape = jax.ShapeDtypeStruct
    piece_shape = [shape((owned, HD, HD), F32)] * group
    unit = 2 * rows * HD * HD * heads

    mine = pl.BlockSpec((rows, width), lambda j, s: (0, s[0] ^ j))
    mine_gain = pl.BlockSpec((1, width), lambda j, s: (0, s[0] ^ j))
    mine_heads = pl.BlockSpec((owned, HD, HD), lambda j, s: (s[0] ^ j, 0, 0))
    whole_piece = pl.BlockSpec((owned, HD, HD), lambda j, s: (0, 0, 0))
    whole_sums = pl.BlockSpec((2 * rows, HD), lambda j, s: (0, 0))
    step_heads = 2 if heads % 2 == 0 else 1
    plain = pl.BlockSpec((rows, step_heads * HD), lambda h: (0, h))
    plain_heads = pl.BlockSpec((step_heads, HD, HD), lambda h: (h, 0, 0))
    plain_grid = (heads // step_heads,)

    def exchange(parts):
        return [parts[0]] + [
            lax.ppermute(parts[j], "seq", [(s, s ^ j) for s in range(peers)])
            for j in range(1, group)
        ]

    def moved(part, by, reverse):
        pairs = [(s, s + by) for s in range(peers - by)]
        return lax.ppermute(part, "seq", [(b, a) for a, b in pairs] if reverse else pairs)

    def exclusive(parts, reverse):
        got = exchange(parts)
        count = peers // group
        carry = jnp.zeros_like(got[0])
        if count > 1:
            carry = moved(functools.reduce(jnp.add, got), group, reverse)
            step = 1
            while step < count - 1:
                carry = carry + moved(carry, group * step, reverse)
                step *= 2
        whole = pl.BlockSpec((owned, HD, HD), lambda j, s: (0, 0, 0))
        back = call(
            functools.partial(owner_kernel, reverse),
            (1,),
            [whole] * (1 + group),
            [whole] * group,
            piece_shape,
            [],
            [spot],
            [carry, *got],
            0,
        )
        return exchange(back)

    totals = call(
        kv_kernel, (group,), [mine] * 2, [whole_piece] * group, piece_shape, [], [spot],
        [key_act, value_act], unit,
    )
    local, scores, states = call(
        local_kernel, plain_grid, [plain] * 3, [plain] * 3,
        [shape((rows, columns), F32)] + [shape((rows, columns), BF16)] * 2, [], [],
        [query_act, key_act, value_act], 4 * unit,
    )
    pieces = exclusive(totals, False)
    attn, sums, far = call(
        functools.partial(norm_kernel, group), (group,),
        [mine, mine, mine, mine_gain] + [whole_piece] * group,
        [mine, whole_sums, mine_heads],
        [shape((rows, columns), F32), shape((2 * rows, HD), F32), shape((heads, HD, HD), BF16)],
        [pltpu.VMEM((width, width), BF16)], [spot],
        [query_act, local, upstream, gain, *pieces], unit,
    )
    every = [sums] + [
        lax.ppermute(sums, "head", [(s, (s + t) % sides) for s in range(sides)])
        for t in range(1, sides)
    ]
    grad, *totals = call(
        functools.partial(grad_kernel, sides, float(columns * sides)), (group,),
        [mine, mine, mine, mine_gain] + [whole_sums] * sides,
        [mine] + [whole_piece] * group,
        [shape((rows, columns), BF16)] + piece_shape,
        [pltpu.VMEM((rows, HD), F32)] * 2, [spot],
        [query_act, attn, upstream, gain, *every], unit,
    )
    grad_q, near_k, near_v = call(
        back_kernel, plain_grid, [plain] * 6 + [plain_heads], [plain] * 3,
        [shape((rows, columns), BF16)] + [shape((rows, columns), F32)] * 2, [], [],
        [query_act, key_act, value_act, grad, scores, states, far], 8 * unit,
    )
    pieces = exclusive(totals, True)
    grad_k, grad_v = call(
        functools.partial(finish_kernel, group), (group,),
        [mine] * 4 + [whole_piece] * group, [mine] * 2,
        [shape((rows, columns), BF16)] * 2, [pltpu.VMEM((width, width), BF16)], [spot],
        [key_act, value_act, near_k, near_v, *pieces], 2 * unit,
    )
    return grad_q, grad_k, grad_v


def solution(mesh):
    spec = P("seq", "head")
    return jax.shard_map(
        on_device, mesh=mesh, in_specs=(spec,) * 4 + (P("head"),), out_specs=(spec,) * 3,
        check_vma=False,
    )
```

```python
import functools

import jax
import jax.numpy as jnp
from jax import lax
from jax.experimental import pallas as pl
from jax.experimental.pallas import tpu as pltpu
from jax.sharding import PartitionSpec as P

HD = 128
CH = 128
F32 = jnp.float32
BF16 = jnp.bfloat16
VMEM_LIMIT = 16 << 20


def group_size(peers, heads):
    size = 1
    while size < 8 and peers % (2 * size) == 0 and heads % (2 * size) == 0:
        size *= 2
    return size


def dot(a, b, a_dim, b_dim):
    return lax.dot_general(a, b, (((a_dim,), (b_dim,)), ((), ())), preferred_element_type=F32)


def head_columns(i):
    return slice(i * HD, (i + 1) * HD)


def causal():
    rows = lax.broadcasted_iota(jnp.int32, (CH, CH), 0)
    columns = lax.broadcasted_iota(jnp.int32, (CH, CH), 1)
    return columns <= rows


def diagonal(blocks):
    if len(blocks) == 1:
        return blocks[0].astype(BF16)
    zero = jnp.zeros((HD, HD), BF16)
    lines = [
        jnp.concatenate([b.astype(BF16) if i == n else zero for n in range(len(blocks))], axis=1)
        for i, b in enumerate(blocks)
    ]
    return jnp.concatenate(lines, axis=0)


def owner_columns(spot, j, width):
    return pl.ds(pl.multiple_of((spot[0] ^ j) * width, width), width)


def kv_kernel(group, owned, spot, k_hbm, v_hbm, *refs):
    outs, (k_buf, v_buf, sems) = refs[:group], refs[group:]
    width = owned * HD
    copies = []
    for j in range(group):
        c = owner_columns(spot, j, width)
        copies.append(
            [
                pltpu.make_async_copy(k_hbm.at[:, c], k_buf.at[j], sems.at[0, j]),
                pltpu.make_async_copy(v_hbm.at[:, c], v_buf.at[j], sems.at[1, j]),
            ]
        )
        for copy in copies[-1]:
            copy.start()
    for j in range(group):
        for copy in copies[j]:
            copy.wait()
        for i in range(owned):
            c = head_columns(i)
            outs[j][i] = dot(k_buf[j, :, c], v_buf[j, :, c], 0, 0)


def local_kernel(step_heads, q_ref, k_ref, v_ref, attn_ref, scores_ref, state_ref):
    rows, columns = q_ref.shape
    blocks = rows // CH
    mask = causal()
    width = step_heads * HD

    def step(h, _):
        for i in range(step_heads):
            c = pl.ds(pl.multiple_of(h * width + i * HD, HD), HD)
            state = jnp.zeros((HD, HD), F32)
            for b in range(blocks):
                r = pl.ds(b * CH, CH)
                q, k, v = q_ref[r, c], k_ref[r, c], v_ref[r, c]
                scores = jnp.where(mask, dot(q, k, 1, 1), 0.0).astype(BF16)
                scores_ref[r, c] = scores
                state_ref[r, c] = state
                attn = dot(scores, v, 1, 0)
                if b:
                    attn = attn + dot(q, state.astype(BF16), 1, 0)
                attn_ref[r, c] = attn
                if b + 1 < blocks:
                    state = state + dot(k, v, 0, 0)
        return 0

    lax.fori_loop(0, columns // width, step, 0)


def total_kernel(count, *refs):
    total = refs[0][...]
    for ref in refs[1:count]:
        total = total + ref[...]
    refs[count][...] = total


def owner_kernel(reverse, count, spot, carry, *refs):
    got, outs = refs[:count], refs[count:]
    me = spot[0]
    for n in range(count):
        part = carry[...]
        for m in range(count):
            inside = (me ^ m) > (me ^ n) if reverse else (me ^ m) < (me ^ n)
            if m != n:
                part = part + jnp.where(inside, got[m][...], 0.0)
        outs[n][...] = part


def norm_kernel(count, spot, q_ref, local_ref, u_ref, gain_ref, *refs):
    pieces, (attn_ref, sums_ref, far_ref) = refs[:count], refs[count:]
    rows = q_ref.shape[0]
    owned = pieces[0].shape[0]
    width = owned * HD
    for j in range(count):
        c = owner_columns(spot, j, width)
        attn = local_ref[:, c] + dot(
            q_ref[:, c], diagonal([pieces[j][i] for i in range(owned)]), 1, 0
        )
        attn_ref[:, c] = attn
        guided = gain_ref[:, c] * u_ref[:, c].astype(F32)
        squares, crossed = attn * attn, guided * attn
        total_sq = sum(squares[:, head_columns(i)] for i in range(owned))
        total_cr = sum(crossed[:, head_columns(i)] for i in range(owned))
        if j:
            sums_ref[:rows] += total_sq
            sums_ref[rows:] += total_cr
        else:
            sums_ref[:rows] = total_sq
            sums_ref[rows:] = total_cr
        for i in range(owned):
            far_ref[(spot[0] ^ j) * owned + i] = pieces[j][i]


def grad_kernel(sums_count, features, group, spot, q_ref, attn_ref, u_ref, gain_ref, *refs):
    sums, g_ref, outs = refs[:sums_count], refs[sums_count], refs[sums_count + 1 :]
    rows = q_ref.shape[0]
    owned = outs[0].shape[0]
    total = sums[0][...]
    for other in sums[1:]:
        total = total + other[...]
    mean = jnp.sum(total, axis=1, keepdims=True) / features
    inverse = lax.rsqrt(mean[:rows] + 1e-06)
    a = jnp.broadcast_to(inverse, (rows, HD))
    b = jnp.broadcast_to(inverse * inverse * inverse * mean[rows:], (rows, HD))
    for j in range(group):
        for i in range(owned):
            c = pl.ds(pl.multiple_of((spot[0] ^ j) * owned * HD + i * HD, HD), HD)
            guided = gain_ref[:, c] * u_ref[:, c].astype(F32)
            grad = (a * guided - b * attn_ref[:, c]).astype(BF16)
            g_ref[:, c] = grad
            outs[j][i] = dot(q_ref[:, c], grad, 0, 0)


def query_kernel(step_heads, k_ref, v_ref, g_ref, state_ref, far_ref, scores_ref, out, buf, sems):
    rows, columns = k_ref.shape
    mask = causal()
    width = step_heads * HD
    steps = columns // width

    def copy(h):
        c = pl.ds(pl.multiple_of(h * width, width), width)
        return pltpu.make_async_copy(buf.at[:, c], out.at[:, c], sems.at[h])

    def step(h, _):
        for i in range(step_heads):
            c = pl.ds(pl.multiple_of(h * width + i * HD, HD), HD)
            far = far_ref[h * step_heads + i]
            for b in range(rows // CH):
                r = pl.ds(b * CH, CH)
                k, g = k_ref[r, c], g_ref[r, c]
                scores = jnp.where(mask, dot(g, v_ref[r, c], 1, 1), 0.0).astype(BF16)
                scores_ref[r, c] = scores
                before = (far + state_ref[r, c]).astype(BF16)
                buf[r, c] = (dot(scores, k, 1, 0) + dot(g, before, 1, 1)).astype(BF16)
        copy(h).start()
        return 0

    lax.fori_loop(0, steps, step, 0)

    def finish(h, _):
        copy(h).wait()
        return 0

    lax.fori_loop(0, steps, finish, 0)


def near_kernel(step_heads, q_ref, k_ref, v_ref, g_ref, fwd_ref, back_ref, gk_ref, gv_ref):
    rows, columns = q_ref.shape
    last = rows // CH - 1
    width = step_heads * HD

    def step(h, _):
        for i in range(step_heads):
            c = pl.ds(pl.multiple_of(h * width + i * HD, HD), HD)
            state = jnp.zeros((HD, HD), F32)
            for b in range(last, -1, -1):
                r = pl.ds(b * CH, CH)
                q, g = q_ref[r, c], g_ref[r, c]
                gk = dot(back_ref[r, c], q, 0, 0)
                gv = dot(fwd_ref[r, c], g, 0, 0)
                if b < last:
                    near = state.astype(BF16)
                    gk = gk + dot(v_ref[r, c], near, 1, 1)
                    gv = gv + dot(k_ref[r, c], near, 1, 0)
                gk_ref[r, c] = gk
                gv_ref[r, c] = gv
                if b:
                    state = state + dot(q, g, 0, 0)
        return 0

    lax.fori_loop(0, columns // width, step, 0)


def finish_kernel(count, spot, k_ref, v_ref, gk_ref, gv_ref, *refs):
    pieces, (gk_out, gv_out, gk_buf, gv_buf, sems) = refs[:count], refs[count:]
    owned = pieces[0].shape[0]
    copies = []
    for j in range(count):
        c = owner_columns(spot, j, owned * HD)
        wide = diagonal([pieces[j][i] for i in range(owned)])
        gk_buf[j] = (gk_ref[:, c] + dot(v_ref[:, c], wide, 1, 1)).astype(BF16)
        copies.append(pltpu.make_async_copy(gk_buf.at[j], gk_out.at[:, c], sems.at[0, j]))
        copies[-1].start()
        gv_buf[j] = (gv_ref[:, c] + dot(k_ref[:, c], wide, 1, 0)).astype(BF16)
        copies.append(pltpu.make_async_copy(gv_buf.at[j], gv_out.at[:, c], sems.at[1, j]))
        copies[-1].start()
    for copy in copies:
        copy.wait()


LOCAL = pl.BlockSpec(memory_space=pltpu.VMEM)
SCALAR = pl.BlockSpec(memory_space=pltpu.SMEM)
FAR = pl.BlockSpec(memory_space=pl.ANY)


def call(kernel, args, in_specs, out_shape, out_specs, scratch=(), flops=0):
    moved = sum(a.size * a.dtype.itemsize for a in args)
    return pl.pallas_call(
        kernel,
        out_shape=out_shape,
        in_specs=in_specs,
        out_specs=out_specs,
        scratch_shapes=list(scratch),
        cost_estimate=pl.CostEstimate(flops=flops, bytes_accessed=moved, transcendentals=0),
        compiler_params=pltpu.CompilerParams(vmem_limit_bytes=VMEM_LIMIT),
    )(*args)


def on_device(query_act, key_act, value_act, upstream, norm_gain):
    peers, sides = lax.axis_size("seq"), lax.axis_size("head")
    rows, columns = query_act.shape
    heads = columns // HD
    group = group_size(peers, heads)
    owned = heads // group
    width = owned * HD
    spot = jnp.reshape(lax.axis_index("seq") % group, (1,)).astype(jnp.int32)
    gain = norm_gain.reshape(1, columns)
    shape = jax.ShapeDtypeStruct
    piece = shape((owned, HD, HD), F32)
    wide = shape((rows, columns), F32)
    half = shape((rows, columns), BF16)
    unit = 2 * rows * HD * HD * heads
    step_heads = 2 if heads % 2 == 0 else 1

    def exchange(parts):
        return [parts[0]] + [
            lax.ppermute(parts[j], "seq", [(s, s ^ j) for s in range(peers)])
            for j in range(1, group)
        ]

    def moved(part, by, reverse):
        pairs = [(s, s + by) for s in range(peers - by)]
        return lax.ppermute(part, "seq", [(b, a) for a, b in pairs] if reverse else pairs)

    def exclusive(parts, reverse, cover):
        got = exchange(parts)
        covered = cover()
        got, covered = lax.optimization_barrier((got, covered))
        count = peers // group
        carry = jnp.zeros_like(got[0])
        if count > 1:
            total = call(
                functools.partial(total_kernel, group), got, [LOCAL] * group, piece, LOCAL
            )
            carry = moved(total, group, reverse)
            step = 1
            while step < count - 1:
                carry = carry + moved(carry, group * step, reverse)
                step *= 2
        back = call(
            functools.partial(owner_kernel, reverse, group),
            [spot, carry, *got], [SCALAR] + [LOCAL] * (1 + group),
            [piece] * group, [LOCAL] * group,
        )
        return exchange(back), covered

    totals = call(
        functools.partial(kv_kernel, group, owned),
        [spot, key_act, value_act], [SCALAR, FAR, FAR], [piece] * group, [LOCAL] * group,
        [pltpu.VMEM((group, rows, width), BF16)] * 2 + [pltpu.SemaphoreType.DMA((2, group))],
        flops=unit,
    )
    pieces, (local, scores, states) = exclusive(
        totals, False,
        lambda: call(
            functools.partial(local_kernel, step_heads),
            [query_act, key_act, value_act], [LOCAL] * 3, [wide, half, wide], [LOCAL] * 3,
            flops=4 * unit,
        ),
    )
    attn, sums, far = call(
        functools.partial(norm_kernel, group),
        [spot, query_act, local, upstream, gain, *pieces], [SCALAR] + [LOCAL] * (4 + group),
        [wide, shape((2 * rows, HD), F32), shape((heads, HD, HD), F32)], [LOCAL] * 3,
        flops=unit,
    )
    every = [sums] + [
        lax.ppermute(sums, "head", [(s, (s + t) % sides) for s in range(sides)])
        for t in range(1, sides)
    ]
    grad, *totals = call(
        functools.partial(grad_kernel, sides, float(columns * sides), group),
        [spot, query_act, attn, upstream, gain, *every], [SCALAR] + [LOCAL] * (4 + sides),
        [half] + [piece] * group, [LOCAL] * (1 + group), flops=unit,
    )
    pieces, (back, grad_q) = exclusive(
        totals, True,
        lambda: call(
            functools.partial(query_kernel, step_heads),
            [key_act, value_act, grad, states, far], [LOCAL] * 5, [half, half], [LOCAL, FAR],
            [pltpu.VMEM((rows, columns), BF16), pltpu.SemaphoreType.DMA((heads // step_heads,))],
            flops=3 * unit,
        ),
    )
    near_k, near_v = call(
        functools.partial(near_kernel, step_heads),
        [query_act, key_act, value_act, grad, scores, back], [LOCAL] * 6, [wide] * 2, [LOCAL] * 2,
        flops=5 * unit,
    )
    grad_k, grad_v = call(
        functools.partial(finish_kernel, group),
        [spot, key_act, value_act, near_k, near_v, *pieces], [SCALAR] + [LOCAL] * (4 + group),
        [half] * 2, [FAR] * 2,
        [pltpu.VMEM((group, rows, width), BF16)] * 2 + [pltpu.SemaphoreType.DMA((2, group))],
        flops=2 * unit,
    )
    return grad_q, grad_k, grad_v


def solution(mesh):
    spec = P("seq", "head")
    return jax.shard_map(
        on_device, mesh=mesh, in_specs=(spec,) * 4 + (P("head"),), out_specs=(spec,) * 3,
        check_vma=False,
    )
```

```python
import functools

import jax
import jax.numpy as jnp
from jax import lax
from jax.experimental import pallas as pl
from jax.experimental.pallas import tpu as pltpu
from jax.sharding import PartitionSpec as P


HD = 128
CH = 128
F32 = jnp.float32
BF16 = jnp.bfloat16
VMEM_LIMIT = 16 << 20
SENDS = (6, 1, 5, 2, 3, 4, 7)
SOON = 5


def group_size(peers, heads):
    size = 1
    while size < 8 and peers % (2 * size) == 0 and heads % (2 * size) == 0:
        size *= 2
    return size


def dot(a, b, a_dim, b_dim):
    return lax.dot_general(a, b, (((a_dim,), (b_dim,)), ((), ())), preferred_element_type=F32)


def head_columns(i):
    return slice(i * HD, (i + 1) * HD)


def causal():
    rows = lax.broadcasted_iota(jnp.int32, (CH, CH), 0)
    columns = lax.broadcasted_iota(jnp.int32, (CH, CH), 1)
    return columns <= rows


def diagonal(blocks):
    if len(blocks) == 1:
        return blocks[0].astype(BF16)
    zero = jnp.zeros((HD, HD), BF16)
    lines = [
        jnp.concatenate([b.astype(BF16) if i == n else zero for n in range(len(blocks))], axis=1)
        for i, b in enumerate(blocks)
    ]
    return jnp.concatenate(lines, axis=0)


def in_hbm(x):
    return pltpu.with_memory_space_constraint(x, pltpu.HBM)


def step_columns(h, step_heads):
    first = h * step_heads * HD
    return [pl.ds(pl.multiple_of(first + i * HD, HD), HD) for i in range(step_heads)]


def owner_columns(spot, j, width, head=None):
    first = (spot[0] ^ j) * width
    if head is None:
        return pl.ds(pl.multiple_of(first, width), width)
    return pl.ds(pl.multiple_of(first + head * HD, HD), HD)


def kv_kernel(group, owned, spot, k_hbm, v_hbm, k_ref, v_ref, state_ref, *refs):
    outs, sems = refs[:group], refs[group]
    columns = [owner_columns(spot, j, owned * HD) for j in range(group)]
    blocks = [pl.ds(b * CH, CH) for b in range(k_ref.shape[0] // CH)]
    copies = []
    for j, c in enumerate(columns):
        copies.append(
            [
                pltpu.make_async_copy(k_hbm.at[:, c], k_ref.at[:, c], sems.at[0, j]),
                pltpu.make_async_copy(v_hbm.at[:, c], v_ref.at[:, c], sems.at[1, j]),
            ]
        )
        for copy in copies[-1]:
            copy.start()
    for j in range(group):
        for copy in copies[j]:
            copy.wait()
        for i in range(owned):
            c = owner_columns(spot, j, owned * HD, i)
            state = jnp.zeros((HD, HD), F32)
            for r in blocks:
                state_ref[r, c] = state
                state = state + dot(k_ref[r, c], v_ref[r, c], 0, 0)
            outs[j][i] = state


def local_kernel(step_heads, first, last, q_ref, k_ref, v_ref, state_ref, *refs):
    attn_ref, scores_ref = refs[-2:]
    mask = causal()
    blocks = [pl.ds(b * CH, CH) for b in range(q_ref.shape[0] // CH)]

    def step(h, _):
        columns = step_columns(h, step_heads)
        for c in columns:
            for r in blocks:
                scores = jnp.where(mask, dot(q_ref[r, c], k_ref[r, c], 1, 1), 0.0)
                scores_ref[r, c] = scores.astype(BF16)
        for c in columns:
            for r in blocks:
                attn = dot(scores_ref[r, c], v_ref[r, c], 1, 0)
                if r is not blocks[0]:
                    attn = attn + dot(q_ref[r, c], state_ref[r, c].astype(BF16), 1, 0)
                attn_ref[r, c] = attn
        return 0

    lax.fori_loop(first, last, step, 0)


def total_kernel(count, *refs):
    total = refs[0][...]
    for ref in refs[1:count]:
        total = total + ref[...]
    refs[count][...] = total


def owner_kernel(reverse, count, spot, carry, *refs):
    got, outs = refs[:count], refs[count:]
    me = spot[0]
    for n in range(count):
        part = carry[...]
        for m in range(count):
            inside = (me ^ m) > (me ^ n) if reverse else (me ^ m) < (me ^ n)
            if m != n:
                part = part + jnp.where(inside, got[m][...], 0.0)
        outs[n][...] = part


def norm_kernel(slots, spot, q_ref, local_ref, u_ref, gain_ref, *refs):
    pieces, before = refs[: len(slots)], refs[len(slots) : -3]
    attn_ref, sums_ref, far_ref = refs[-3:]
    rows = q_ref.shape[0]
    owned = pieces[0].shape[0]
    for n, j in enumerate(slots):
        c = owner_columns(spot, j, owned * HD)
        attn = local_ref[:, c] + dot(
            q_ref[:, c], diagonal([pieces[n][i] for i in range(owned)]), 1, 0
        )
        attn_ref[:, c] = attn
        guided = gain_ref[:, c] * u_ref[:, c].astype(F32)
        squares, crossed = attn * attn, guided * attn
        total_sq = sum(squares[:, head_columns(i)] for i in range(owned))
        total_cr = sum(crossed[:, head_columns(i)] for i in range(owned))
        sums = sums_ref if n else (before[1] if before else None)
        if sums is not None:
            total_sq = total_sq + sums[:rows]
            total_cr = total_cr + sums[rows:]
        sums_ref[:rows] = total_sq
        sums_ref[rows:] = total_cr
        for i in range(owned):
            far_ref[(spot[0] ^ j) * owned + i] = pieces[n][i]


def grad_kernel(sums_count, features, group, spot, q_ref, attn_ref, u_ref, gain_ref, *refs):
    sums, g_ref, outs = refs[:sums_count], refs[sums_count], refs[sums_count + 1 :]
    rows = q_ref.shape[0]
    owned = outs[0].shape[0]
    total = sums[0][...]
    for other in sums[1:]:
        total = total + other[...]
    mean = jnp.sum(total, axis=1, keepdims=True) / features
    inverse = lax.rsqrt(mean[:rows] + 1e-06)
    a = jnp.broadcast_to(inverse, (rows, HD))
    b = jnp.broadcast_to(inverse * inverse * inverse * mean[rows:], (rows, HD))
    for j in range(group):
        for i in range(owned):
            c = pl.ds(pl.multiple_of((spot[0] ^ j) * owned * HD + i * HD, HD), HD)
            guided = gain_ref[:, c] * u_ref[:, c].astype(F32)
            grad = (a * guided - b * attn_ref[:, c]).astype(BF16)
            g_ref[:, c] = grad
            outs[j][i] = dot(q_ref[:, c], grad, 0, 0)


def query_kernel(step_heads, first, last, k_ref, v_ref, g_ref, state_ref, far_ref, *refs):
    scores_ref, gq_ref = refs[-2:]
    mask = causal()
    blocks = [pl.ds(b * CH, CH) for b in range(k_ref.shape[0] // CH)]

    def step(h, _):
        columns = step_columns(h, step_heads)
        for c in columns:
            for r in blocks:
                scores = jnp.where(mask, dot(g_ref[r, c], v_ref[r, c], 1, 1), 0.0)
                scores_ref[r, c] = scores.astype(BF16)
        for i, c in enumerate(columns):
            far = far_ref[h * step_heads + i]
            for r in blocks:
                before = (far + state_ref[r, c]).astype(BF16)
                gq = dot(scores_ref[r, c], k_ref[r, c], 1, 0) + dot(g_ref[r, c], before, 1, 1)
                gq_ref[r, c] = gq.astype(BF16)
        return 0

    lax.fori_loop(first, last, step, 0)


def near_kernel(step_heads, first, last, q_ref, k_ref, v_ref, g_ref, fwd_ref, back_ref, gq_ref, *refs):
    gk_ref, gv_ref, gq_out, states, sem = refs[-5:]
    width = step_heads * HD
    mine = pl.ds(first * width, (last - first) * width)
    copy = pltpu.make_async_copy(gq_ref.at[:, mine], gq_out.at[:, mine], sem)
    copy.start()
    blocks = [pl.ds(b * CH, CH) for b in range(q_ref.shape[0] // CH)]

    def step(h, _):
        columns = step_columns(h, step_heads)
        for i, c in enumerate(columns):
            state = jnp.zeros((HD, HD), F32)
            for r in blocks[:0:-1]:
                state = state + dot(q_ref[r, c], g_ref[r, c], 0, 0)
                states[r, head_columns(i)] = state.astype(BF16)
        for i, c in enumerate(columns):
            for n, r in enumerate(blocks):
                gk = dot(back_ref[r, c], q_ref[r, c], 0, 0)
                gv = dot(fwd_ref[r, c], g_ref[r, c], 0, 0)
                if n + 1 < len(blocks):
                    near = states[blocks[n + 1], head_columns(i)]
                    gk = gk + dot(v_ref[r, c], near, 1, 1)
                    gv = gv + dot(k_ref[r, c], near, 1, 0)
                gk_ref[r, c] = gk
                gv_ref[r, c] = gv
        return 0

    lax.fori_loop(first, last, step, 0)
    copy.wait()


def finish_kernel(slots, spot, k_ref, v_ref, gk_ref, gv_ref, *refs):
    pieces, (gk_out, gv_out, gk_buf, gv_buf, sems) = refs[: len(slots)], refs[-5:]
    owned = pieces[0].shape[0]
    copies = []
    for n, j in enumerate(slots):
        c = owner_columns(spot, j, owned * HD)
        wide = diagonal([pieces[n][i] for i in range(owned)])
        gk_buf[n] = (gk_ref[:, c] + dot(v_ref[:, c], wide, 1, 1)).astype(BF16)
        copies.append(pltpu.make_async_copy(gk_buf.at[n], gk_out.at[:, c], sems.at[0, n]))
        copies[-1].start()
        gv_buf[n] = (gv_ref[:, c] + dot(k_ref[:, c], wide, 1, 0)).astype(BF16)
        copies.append(pltpu.make_async_copy(gv_buf.at[n], gv_out.at[:, c], sems.at[1, n]))
        copies[-1].start()
    for copy in copies:
        copy.wait()


LOCAL = pl.BlockSpec(memory_space=pltpu.VMEM)
SCALAR = pl.BlockSpec(memory_space=pltpu.SMEM)
FAR = pl.BlockSpec(memory_space=pltpu.HBM)


def call(kernel, args, in_specs, out_shape, out_specs, scratch=(), flops=0, aliases=None):
    moved = sum(a.size * a.dtype.itemsize for a in args)
    return pl.pallas_call(
        kernel,
        out_shape=out_shape,
        in_specs=in_specs,
        out_specs=out_specs,
        scratch_shapes=list(scratch),
        input_output_aliases=aliases or {},
        cost_estimate=pl.CostEstimate(flops=flops, bytes_accessed=moved, transcendentals=0),
        compiler_params=pltpu.CompilerParams(vmem_limit_bytes=VMEM_LIMIT),
    )(*args)


def on_device(query_act, key_act, value_act, upstream, norm_gain):
    peers, sides = lax.axis_size("seq"), lax.axis_size("head")
    rows, columns = query_act.shape
    heads = columns // HD
    group = group_size(peers, heads)
    owned = heads // group
    width = owned * HD
    spot = jnp.reshape(lax.axis_index("seq") % group, (1,)).astype(jnp.int32)
    gain = norm_gain.reshape(1, columns)
    shape = jax.ShapeDtypeStruct
    piece = shape((owned, HD, HD), F32)
    wide = shape((rows, columns), F32)
    half = shape((rows, columns), BF16)
    unit = 2 * rows * HD * HD * heads
    step_heads = next(n for n in (4, 2, 1) if heads % n == 0)
    steps = heads // step_heads

    def pieces_of(count, kernel, args, in_specs, out_shape, out_specs, scratch, flops):
        outs = None
        count = min(count, steps)
        for n in range(count):
            first, last = n * steps // count, (n + 1) * steps // count
            more = [] if outs is None else list(outs)
            outs = call(
                functools.partial(kernel, step_heads, first, last),
                [*args, *more], [*in_specs, *out_specs[: len(more)]], out_shape, out_specs,
                scratch, flops // count, {len(args) + i: i for i in range(len(more))},
            )
        return outs

    def exchange(parts):
        out = [parts[0]] + [None] * (group - 1)
        order = [j for j in SENDS if j < group]
        for j in order:
            out[j] = lax.ppermute(parts[j], "seq", [(s, s ^ j) for s in range(peers)])
        return out

    def moved(part, by, reverse):
        pairs = [(s, s + by) for s in range(peers - by)]
        return lax.ppermute(part, "seq", [(b, a) for a, b in pairs] if reverse else pairs)

    def exclusive(parts, reverse):
        got = exchange(parts)
        groups = peers // group
        carry = jnp.zeros_like(got[0])
        if groups > 1:
            total = call(
                functools.partial(total_kernel, group), got, [LOCAL] * group, piece, LOCAL
            )
            carry = moved(total, group, reverse)
            step = 1
            while step < groups - 1:
                carry = carry + moved(carry, group * step, reverse)
                step *= 2
        back = call(
            functools.partial(owner_kernel, reverse, group),
            [spot, carry, *got], [SCALAR] + [LOCAL] * (1 + group),
            [piece] * group, [LOCAL] * group,
        )
        return exchange(back)

    slots = [j for j in (0, *SENDS) if j < group]
    halves = [h for h in (slots[: SOON], slots[SOON :]) if h]

    def halves_of(kernel, args, in_specs, out_shape, out_specs, scratch, flops):
        outs = None
        for half in halves:
            more = [] if outs is None else list(outs)
            at = len(args) + len(half)
            outs = call(
                functools.partial(kernel, half),
                [*args, *(pieces[j] for j in half), *more],
                [*in_specs, *[LOCAL] * len(half), *out_specs[: len(more)]],
                out_shape, out_specs, scratch, flops * len(half) // group,
                {at + i: i for i in range(len(more))},
            )
        return outs

    key_near, value_near, states, *totals = call(
        functools.partial(kv_kernel, group, owned),
        [spot, in_hbm(key_act), in_hbm(value_act)], [SCALAR, FAR, FAR], [half, half, wide] + [piece] * group,
        [LOCAL] * (3 + group), [pltpu.SemaphoreType.DMA((2, group))], flops=unit,
    )
    local, scores = pieces_of(
        2, local_kernel, [query_act, key_near, value_near, states], [LOCAL] * 4,
        [wide, half], [LOCAL] * 2, (), 3 * unit,
    )
    pieces = exclusive(totals, False)
    attn, sums, far = halves_of(
        norm_kernel, [spot, query_act, local, upstream, gain], [SCALAR] + [LOCAL] * 4,
        [wide, shape((2 * rows, HD), F32), shape((heads, HD, HD), F32)], [LOCAL] * 3, (), unit,
    )
    every = [sums] + [
        lax.ppermute(sums, "head", [(s, (s + t) % sides) for s in range(sides)])
        for t in range(1, sides)
    ]
    grad, *totals = call(
        functools.partial(grad_kernel, sides, float(columns * sides), group),
        [spot, query_act, attn, upstream, gain, *every], [SCALAR] + [LOCAL] * (4 + sides),
        [half] + [piece] * group, [LOCAL] * (1 + group), flops=unit,
    )
    back, near_q = pieces_of(
        1, query_kernel, [key_near, value_near, grad, states, far], [LOCAL] * 5,
        [half, half], [LOCAL] * 2, (), 3 * unit,
    )
    near_k, near_v, grad_q = pieces_of(
        1, near_kernel, [query_act, key_near, value_near, grad, scores, back, near_q],
        [LOCAL] * 7, [wide, wide, half], [LOCAL, LOCAL, FAR],
        [pltpu.VMEM((rows, step_heads * HD), BF16), pltpu.SemaphoreType.DMA],
        5 * unit,
    )
    pieces = exclusive(totals, True)
    most = max(len(h) for h in halves)
    grad_k, grad_v = halves_of(
        finish_kernel, [spot, key_near, value_near, near_k, near_v],
        [SCALAR] + [LOCAL] * 4, [half] * 2, [FAR] * 2,
        [pltpu.VMEM((most, rows, width), BF16)] * 2 + [pltpu.SemaphoreType.DMA((2, most))],
        2 * unit,
    )
    return grad_q, grad_k, grad_v


def solution(mesh):
    spec = P("seq", "head")

    return jax.shard_map(
        on_device, mesh=mesh, in_specs=(spec,) * 4 + (P("head"),), out_specs=(spec,) * 3,
        check_vma=False,
    )
```

```python
import functools
import math

import jax
import jax.numpy as jnp
from jax import lax
from jax.experimental import pallas as pl
from jax.experimental.pallas import tpu as pltpu
from jax.sharding import PartitionSpec as P


HD = 128
CH = 128
F32 = jnp.float32
BF16 = jnp.bfloat16
VMEM_LIMIT = 16 << 20
SENDS = (5, 2, 6, 1, 4, 3, 7)
PARTS = (7,)


def group_size(peers, heads):
    size = 1
    while size < 8 and peers % (2 * size) == 0 and heads % (2 * size) == 0:
        size *= 2
    return size


def dot(a, b, a_dim, b_dim):
    return lax.dot_general(a, b, (((a_dim,), (b_dim,)), ((), ())), preferred_element_type=F32)


def head_columns(i):
    return slice(i * HD, (i + 1) * HD)


def causal():
    rows = lax.broadcasted_iota(jnp.int32, (CH, CH), 0)
    columns = lax.broadcasted_iota(jnp.int32, (CH, CH), 1)
    return columns <= rows


def diagonal(blocks):
    if len(blocks) == 1:
        return blocks[0].astype(BF16)
    zero = jnp.zeros((HD, HD), BF16)
    lines = [
        jnp.concatenate([b.astype(BF16) if i == n else zero for n in range(len(blocks))], axis=1)
        for i, b in enumerate(blocks)
    ]
    return jnp.concatenate(lines, axis=0)


def in_hbm(x):
    return pltpu.with_memory_space_constraint(x, pltpu.HBM)


def step_columns(h, step_heads):
    first = h * step_heads * HD
    return [pl.ds(pl.multiple_of(first + i * HD, HD), HD) for i in range(step_heads)]


def head_of(spot, n, owned):
    return (spot[0] ^ (n // owned)) * owned + n % owned


def columns_of(head, count=1):
    return pl.ds(pl.multiple_of(head * HD, count * HD), count * HD)


def lot_columns(spot, owned, lot, n):
    return columns_of(head_of(spot, n * lot, owned), lot), columns_of(n * lot, lot)


def fetch(spot, owned, lot, n, far, near, sem):
    there, here = lot_columns(spot, owned, lot, n)
    return pltpu.make_async_copy(far.at[:, there], near.at[:, here], sem)


def kv_kernel(group, owned, spot, k_hbm, v_hbm, k_ref, v_ref, *refs):
    outs, sems = refs[:group], refs[group]
    copies = []
    for j in range(group):
        copies.append(
            [
                fetch(spot, owned, owned, j, k_hbm, k_ref, sems.at[0, j]),
                fetch(spot, owned, owned, j, v_hbm, v_ref, sems.at[1, j]),
            ]
        )
        for copy in copies[-1]:
            copy.start()
    for n in range(group * owned):
        if n % owned == 0:
            for copy in copies[n // owned]:
                copy.wait()
        c = head_columns(n)
        outs[n // owned][n % owned] = dot(k_ref[:, c], v_ref[:, c], 0, 0)


def local_kernel(step_heads, first, last, owned, spot, q_hbm, u_hbm, k_ref, v_ref, *refs):
    attn_ref, scores_ref, state_ref, q_ref, u_ref, sems = refs[-6:]
    mask = causal()

    lot = math.gcd(owned, step_heads)
    lots = step_heads // lot

    def get_q(n):
        return fetch(spot, owned, lot, n, q_hbm, q_ref, sems.at[0, n])

    def get_u(n):
        return fetch(spot, owned, lot, n, u_hbm, u_ref, sems.at[1, n])

    mine = range(first * lots, last * lots)
    for get in (get_q, get_u):
        for n in mine:
            get(n).start()
    blocks = [pl.ds(b * CH, CH) for b in range(q_ref.shape[0] // CH)]

    def step(h, _):
        columns = step_columns(h, step_heads)
        for c in columns:
            state = jnp.zeros((HD, HD), F32)
            for r in blocks:
                state_ref[r, c] = state
                if r is not blocks[-1]:
                    state = state + dot(k_ref[r, c], v_ref[r, c], 0, 0)
        for i in range(lots):
            get_q(h * lots + i).wait()
        for c in columns:
            for r in blocks:
                scores = jnp.where(mask, dot(q_ref[r, c], k_ref[r, c], 1, 1), 0.0)
                scores_ref[r, c] = scores.astype(BF16)
        for c in columns:
            for r in blocks:
                attn = dot(scores_ref[r, c], v_ref[r, c], 1, 0)
                if r is not blocks[0]:
                    attn = attn + dot(q_ref[r, c], state_ref[r, c].astype(BF16), 1, 0)
                attn_ref[r, c] = attn
        return 0

    lax.fori_loop(first, last, step, 0)
    for n in mine:
        get_u(n).wait()


def total_kernel(count, *refs):
    total = refs[0][...]
    for ref in refs[1:count]:
        total = total + ref[...]
    refs[count][...] = total


def owner_kernel(reverse, count, spot, carry, *refs):
    got, outs = refs[:count], refs[count:]
    me = spot[0]
    for n in range(count):
        part = carry[...]
        for m in range(count):
            inside = (me ^ m) > (me ^ n) if reverse else (me ^ m) < (me ^ n)
            if m != n:
                part = part + jnp.where(inside, got[m][...], 0.0)
        outs[n][...] = part


def norm_kernel(slots, spot, q_ref, local_ref, u_ref, gain_ref, *refs):
    pieces, before = refs[: len(slots)], refs[len(slots) : -3]
    attn_ref, sums_ref, far_ref = refs[-3:]
    rows = q_ref.shape[0]
    owned = pieces[0].shape[0]
    for n, j in enumerate(slots):
        c = slice(j * owned * HD, (j + 1) * owned * HD)
        gain = jnp.concatenate(
            [gain_ref[:, columns_of(head_of(spot, j * owned + i, owned))] for i in range(owned)],
            axis=1,
        )
        attn = local_ref[:, c] + dot(
            q_ref[:, c], diagonal([pieces[n][i] for i in range(owned)]), 1, 0
        )
        attn_ref[:, c] = attn
        guided = gain * u_ref[:, c].astype(F32)
        squares, crossed = attn * attn, guided * attn
        total_sq = sum(squares[:, head_columns(i)] for i in range(owned))
        total_cr = sum(crossed[:, head_columns(i)] for i in range(owned))
        sums = sums_ref if n else (before[1] if before else None)
        if sums is not None:
            total_sq = total_sq + sums[:rows]
            total_cr = total_cr + sums[rows:]
        sums_ref[:rows] = total_sq
        sums_ref[rows:] = total_cr
        for i in range(owned):
            far_ref[j * owned + i] = pieces[n][i]


def grad_kernel(sums_count, features, group, spot, q_ref, attn_ref, u_ref, gain_ref, *refs):
    sums, g_ref, outs = refs[:sums_count], refs[sums_count], refs[sums_count + 1 :]
    rows = q_ref.shape[0]
    owned = outs[0].shape[0]
    total = sums[0][...]
    for other in sums[1:]:
        total = total + other[...]
    mean = jnp.sum(total, axis=1, keepdims=True) / features
    inverse = lax.rsqrt(mean[:rows] + 1e-06)
    a = jnp.broadcast_to(inverse, (rows, HD))
    b = jnp.broadcast_to(inverse * inverse * inverse * mean[rows:], (rows, HD))
    for n in range(group * owned):
        c = head_columns(n)
        gain = gain_ref[:, columns_of(head_of(spot, n, owned))]
        guided = gain * u_ref[:, c].astype(F32)
        grad = (a * guided - b * attn_ref[:, c]).astype(BF16)
        g_ref[:, c] = grad
        outs[n // owned][n % owned] = dot(q_ref[:, c], grad, 0, 0)


def query_kernel(step_heads, first, last, k_ref, v_ref, g_ref, state_ref, far_ref, *refs):
    scores_ref, gq_ref = refs[-2:]
    mask = causal()
    blocks = [pl.ds(b * CH, CH) for b in range(k_ref.shape[0] // CH)]

    def step(h, _):
        columns = step_columns(h, step_heads)
        for c in columns:
            for r in blocks:
                scores = jnp.where(mask, dot(g_ref[r, c], v_ref[r, c], 1, 1), 0.0)
                scores_ref[r, c] = scores.astype(BF16)
        for i, c in enumerate(columns):
            far = far_ref[h * step_heads + i]
            for r in blocks:
                before = (far + state_ref[r, c]).astype(BF16)
                gq = dot(scores_ref[r, c], k_ref[r, c], 1, 0) + dot(g_ref[r, c], before, 1, 1)
                gq_ref[r, c] = gq.astype(BF16)
        return 0

    lax.fori_loop(first, last, step, 0)


def near_kernel(step_heads, first, last, owned, spot, q_ref, k_ref, v_ref, g_ref, fwd_ref, back_ref, gq_ref, *refs):
    gk_ref, gv_ref, gq_out, states, sems = refs[-5:]
    lot = math.gcd(owned, step_heads)
    copies = []
    for n in range(first * step_heads // lot, last * step_heads // lot):
        there, here = lot_columns(spot, owned, lot, n)
        copies.append(pltpu.make_async_copy(gq_ref.at[:, here], gq_out.at[:, there], sems.at[n]))
    for copy in copies:
        copy.start()
    blocks = [pl.ds(b * CH, CH) for b in range(q_ref.shape[0] // CH)]

    def step(h, _):
        columns = step_columns(h, step_heads)
        for i, c in enumerate(columns):
            state = jnp.zeros((HD, HD), F32)
            for r in blocks[:0:-1]:
                state = state + dot(q_ref[r, c], g_ref[r, c], 0, 0)
                states[r, head_columns(i)] = state.astype(BF16)
        for i, c in enumerate(columns):
            for n, r in enumerate(blocks):
                gk = dot(back_ref[r, c], q_ref[r, c], 0, 0)
                gv = dot(fwd_ref[r, c], g_ref[r, c], 0, 0)
                if n + 1 < len(blocks):
                    near = states[blocks[n + 1], head_columns(i)]
                    gk = gk + dot(v_ref[r, c], near, 1, 1)
                    gv = gv + dot(k_ref[r, c], near, 1, 0)
                gk_ref[r, c] = gk
                gv_ref[r, c] = gv
        return 0

    lax.fori_loop(first, last, step, 0)
    for copy in copies:
        copy.wait()


def finish_kernel(slots, spot, k_ref, v_ref, gk_ref, gv_ref, *refs):
    pieces, (gk_out, gv_out, gk_buf, gv_buf, sems) = refs[: len(slots)], refs[-5:]
    owned = pieces[0].shape[0]
    copies = []
    for n, j in enumerate(slots):
        c = slice(j * owned * HD, (j + 1) * owned * HD)
        out = pl.ds(pl.multiple_of((spot[0] ^ j) * owned * HD, owned * HD), owned * HD)
        wide = diagonal([pieces[n][i] for i in range(owned)])
        gk_buf[n] = (gk_ref[:, c] + dot(v_ref[:, c], wide, 1, 1)).astype(BF16)
        copies.append(pltpu.make_async_copy(gk_buf.at[n], gk_out.at[:, out], sems.at[0, n]))
        copies[-1].start()
        gv_buf[n] = (gv_ref[:, c] + dot(k_ref[:, c], wide, 1, 0)).astype(BF16)
        copies.append(pltpu.make_async_copy(gv_buf.at[n], gv_out.at[:, out], sems.at[1, n]))
        copies[-1].start()
    for copy in copies:
        copy.wait()


LOCAL = pl.BlockSpec(memory_space=pltpu.VMEM)
SCALAR = pl.BlockSpec(memory_space=pltpu.SMEM)
FAR = pl.BlockSpec(memory_space=pltpu.HBM)


def call(kernel, args, in_specs, out_shape, out_specs, scratch=(), flops=0, aliases=None):
    moved = sum(a.size * a.dtype.itemsize for a in args)
    return pl.pallas_call(
        kernel,
        out_shape=out_shape,
        in_specs=in_specs,
        out_specs=out_specs,
        scratch_shapes=list(scratch),
        input_output_aliases=aliases or {},
        cost_estimate=pl.CostEstimate(flops=flops, bytes_accessed=moved, transcendentals=0),
        compiler_params=pltpu.CompilerParams(vmem_limit_bytes=VMEM_LIMIT),
    )(*args)


def on_device(query_act, key_act, value_act, upstream, norm_gain):
    peers, sides = lax.axis_size("seq"), lax.axis_size("head")
    rows, columns = query_act.shape
    heads = columns // HD
    group = group_size(peers, heads)
    owned = heads // group
    width = owned * HD
    spot = jnp.reshape(lax.axis_index("seq") % group, (1,)).astype(jnp.int32)
    gain = norm_gain.reshape(1, columns)
    shape = jax.ShapeDtypeStruct
    piece = shape((owned, HD, HD), F32)
    wide = shape((rows, columns), F32)
    half = shape((rows, columns), BF16)
    unit = 2 * rows * HD * HD * heads
    step_heads = next(n for n in (4, 2, 1) if heads % n == 0)
    steps = heads // step_heads

    def pieces_of(count, kernel, args, in_specs, out_shape, out_specs, scratch, flops, *more_static):
        outs = None
        count = min(count, steps)
        for n in range(count):
            first, last = n * steps // count, (n + 1) * steps // count
            more = [] if outs is None else list(outs)
            outs = call(
                functools.partial(kernel, step_heads, first, last, *more_static),
                [*args, *more], [*in_specs, *out_specs[: len(more)]], out_shape, out_specs,
                scratch, flops // count, {len(args) + i: i for i in range(len(more))},
            )
        return outs

    def exchange(parts):
        out = [parts[0]] + [None] * (group - 1)
        order = [j for j in SENDS if j < group]
        for j in order:
            out[j] = lax.ppermute(parts[j], "seq", [(s, s ^ j) for s in range(peers)])
        return out

    def moved(part, by, reverse):
        pairs = [(s, s + by) for s in range(peers - by)]
        return lax.ppermute(part, "seq", [(b, a) for a, b in pairs] if reverse else pairs)

    def exclusive(parts, reverse):
        got = exchange(parts)
        groups = peers // group
        carry = jnp.zeros_like(got[0])
        if groups > 1:
            total = call(
                functools.partial(total_kernel, group), got, [LOCAL] * group, piece, LOCAL
            )
            carry = moved(total, group, reverse)
            step = 1
            while step < groups - 1:
                carry = carry + moved(carry, group * step, reverse)
                step *= 2
        back = call(
            functools.partial(owner_kernel, reverse, group),
            [spot, carry, *got], [SCALAR] + [LOCAL] * (1 + group),
            [piece] * group, [LOCAL] * group,
        )
        return exchange(back)

    slots = [j for j in (0, *SENDS) if j < group]
    parts_of = [slots[a:b] for a, b in zip((0, *PARTS), (*PARTS, group)) if slots[a:b]]

    def by_arrival(kernel, args, in_specs, out_shape, out_specs, scratch, flops):
        outs = None
        for some in parts_of:
            more = [] if outs is None else list(outs)
            at = len(args) + len(some)
            outs = call(
                functools.partial(kernel, some),
                [*args, *(pieces[j] for j in some), *more],
                [*in_specs, *[LOCAL] * len(some), *out_specs[: len(more)]],
                out_shape, out_specs, scratch, flops * len(some) // group,
                {at + i: i for i in range(len(more))},
            )
        return outs

    key_near, value_near, *totals = call(
        functools.partial(kv_kernel, group, owned),
        [spot, in_hbm(key_act), in_hbm(value_act)], [SCALAR, FAR, FAR], [half, half] + [piece] * group,
        [LOCAL] * (2 + group), [pltpu.SemaphoreType.DMA((2, heads))], flops=unit,
    )
    local, scores, states, query_near, up_near = pieces_of(
        1, local_kernel,
        [spot, in_hbm(query_act), in_hbm(upstream), key_near, value_near],
        [SCALAR, FAR, FAR] + [LOCAL] * 2, [wide, half, wide, half, half], [LOCAL] * 5,
        [pltpu.SemaphoreType.DMA((2, heads))], 3 * unit, owned,
    )
    pieces = exclusive(totals, False)
    attn, sums, far = by_arrival(
        norm_kernel, [spot, query_near, local, up_near, gain], [SCALAR] + [LOCAL] * 4,
        [wide, shape((2 * rows, HD), F32), shape((heads, HD, HD), F32)], [LOCAL] * 3, (), unit,
    )
    every = [sums] + [
        lax.ppermute(sums, "head", [(s, (s + t) % sides) for s in range(sides)])
        for t in range(1, sides)
    ]
    grad, *totals = call(
        functools.partial(grad_kernel, sides, float(columns * sides), group),
        [spot, query_near, attn, up_near, gain, *every], [SCALAR] + [LOCAL] * (4 + sides),
        [half] + [piece] * group, [LOCAL] * (1 + group), flops=unit,
    )
    back, near_q = pieces_of(
        1, query_kernel, [key_near, value_near, grad, states, far], [LOCAL] * 5,
        [half, half], [LOCAL] * 2, (), 3 * unit,
    )
    near_k, near_v, grad_q = pieces_of(
        1, near_kernel,
        [spot, query_near, key_near, value_near, grad, scores, back, near_q],
        [SCALAR] + [LOCAL] * 7, [wide, wide, half], [LOCAL, LOCAL, FAR],
        [pltpu.VMEM((rows, step_heads * HD), BF16), pltpu.SemaphoreType.DMA((heads,))],
        5 * unit, owned,
    )
    pieces = exclusive(totals, True)
    most = max(len(p) for p in parts_of)
    grad_k, grad_v = by_arrival(
        finish_kernel, [spot, key_near, value_near, near_k, near_v],
        [SCALAR] + [LOCAL] * 4, [half] * 2, [FAR] * 2,
        [pltpu.VMEM((most, rows, width), BF16)] * 2 + [pltpu.SemaphoreType.DMA((2, most))],
        2 * unit,
    )
    return grad_q, grad_k, grad_v


def solution(mesh):
    spec = P("seq", "head")

    return jax.shard_map(
        on_device, mesh=mesh, in_specs=(spec,) * 4 + (P("head"),), out_specs=(spec,) * 3,
        check_vma=False,
    )
```

```python
import functools
import math

import jax
import jax.numpy as jnp
from jax import lax
from jax.experimental import pallas as pl
from jax.experimental.pallas import tpu as pltpu
from jax.sharding import PartitionSpec as P


HD = 128
CH = 128
F32 = jnp.float32
BF16 = jnp.bfloat16
VMEM_LIMIT = 16 << 20
SENDS = (5, 2, 6, 1, 4, 3, 7)
PARTS = (7,)


def group_size(peers, heads):
    size = 1
    while size < 8 and peers % (2 * size) == 0 and heads % (2 * size) == 0:
        size *= 2
    return size


def dot(a, b, a_dim, b_dim):
    return lax.dot_general(a, b, (((a_dim,), (b_dim,)), ((), ())), preferred_element_type=F32)


def head_columns(i):
    return slice(i * HD, (i + 1) * HD)


def causal():
    rows = lax.broadcasted_iota(jnp.int32, (CH, CH), 0)
    columns = lax.broadcasted_iota(jnp.int32, (CH, CH), 1)
    return columns <= rows


def diagonal(blocks):
    if len(blocks) == 1:
        return blocks[0].astype(BF16)
    zero = jnp.zeros((HD, HD), BF16)
    lines = [
        jnp.concatenate([b.astype(BF16) if i == n else zero for n in range(len(blocks))], axis=1)
        for i, b in enumerate(blocks)
    ]
    return jnp.concatenate(lines, axis=0)


def in_hbm(x):
    return pltpu.with_memory_space_constraint(x, pltpu.HBM)


def step_columns(h, step_heads):
    first = h * step_heads * HD
    return [pl.ds(pl.multiple_of(first + i * HD, HD), HD) for i in range(step_heads)]


def head_of(spot, n, owned):
    return (spot[0] ^ (n // owned)) * owned + n % owned


def columns_of(head, count=1):
    return pl.ds(pl.multiple_of(head * HD, count * HD), count * HD)


def lot_columns(spot, owned, lot, n):
    return columns_of(head_of(spot, n * lot, owned), lot), columns_of(n * lot, lot)


def fetch(spot, owned, lot, n, far, near, sem):
    there, here = lot_columns(spot, owned, lot, n)
    return pltpu.make_async_copy(far.at[:, there], near.at[:, here], sem)


def kv_kernel(group, owned, spot, k_hbm, v_hbm, k_ref, v_ref, *refs):
    outs, sems = refs[:group], refs[group]
    copies = []
    for j in range(group):
        copies.append(
            [
                fetch(spot, owned, owned, j, k_hbm, k_ref, sems.at[0, j]),
                fetch(spot, owned, owned, j, v_hbm, v_ref, sems.at[1, j]),
            ]
        )
        for copy in copies[-1]:
            copy.start()
    for n in range(group * owned):
        if n % owned == 0:
            for copy in copies[n // owned]:
                copy.wait()
        c = head_columns(n)
        outs[n // owned][n % owned] = dot(k_ref[:, c], v_ref[:, c], 0, 0)


def local_kernel(step_heads, first, last, owned, spot, q_hbm, u_hbm, k_ref, v_ref, *refs):
    attn_ref, scores_ref, state_ref, q_ref, u_ref, sems = refs[-6:]
    mask = causal()

    lot = math.gcd(owned, step_heads)
    lots = step_heads // lot

    def get_q(n):
        return fetch(spot, owned, lot, n, q_hbm, q_ref, sems.at[0, n])

    def get_u(n):
        return fetch(spot, owned, lot, n, u_hbm, u_ref, sems.at[1, n])

    mine = range(first * lots, last * lots)
    for get in (get_q, get_u):
        for n in mine:
            get(n).start()
    blocks = [pl.ds(b * CH, CH) for b in range(q_ref.shape[0] // CH)]

    def step(h, _):
        columns = step_columns(h, step_heads)
        for c in columns:
            state = jnp.zeros((HD, HD), F32)
            for r in blocks:
                state_ref[r, c] = state
                if r is not blocks[-1]:
                    state = state + dot(k_ref[r, c], v_ref[r, c], 0, 0)
        for i in range(lots):
            get_q(h * lots + i).wait()
        for c in columns:
            for r in blocks:
                scores = jnp.where(mask, dot(q_ref[r, c], k_ref[r, c], 1, 1), 0.0)
                scores_ref[r, c] = scores.astype(BF16)
        for c in columns:
            for r in blocks:
                attn = dot(scores_ref[r, c], v_ref[r, c], 1, 0)
                if r is not blocks[0]:
                    attn = attn + dot(q_ref[r, c], state_ref[r, c].astype(BF16), 1, 0)
                attn_ref[r, c] = attn
        return 0

    lax.fori_loop(first, last, step, 0)
    for n in mine:
        get_u(n).wait()


def total_kernel(count, *refs):
    total = refs[0][...]
    for ref in refs[1:count]:
        total = total + ref[...]
    refs[count][...] = total


def owner_kernel(reverse, count, spot, carry, *refs):
    got, outs = refs[:count], refs[count:]
    me = spot[0]
    for n in range(count):
        part = carry[...]
        for m in range(count):
            inside = (me ^ m) > (me ^ n) if reverse else (me ^ m) < (me ^ n)
            if m != n:
                part = part + jnp.where(inside, got[m][...], 0.0)
        outs[n][...] = part


def first_lanes(rows):
    return lax.broadcasted_iota(jnp.int32, (rows, HD), 1) < HD // 2


def norm_kernel(final, slots, spot, q_ref, local_ref, u_ref, gain_ref, *refs):
    pieces, before = refs[: len(slots)], refs[len(slots) : -4]
    attn_ref, sums_ref, far_ref, fold_ref = refs[-4:]
    rows = q_ref.shape[0]
    owned = pieces[0].shape[0]
    for n, j in enumerate(slots):
        c = slice(j * owned * HD, (j + 1) * owned * HD)
        gain = jnp.concatenate(
            [gain_ref[:, columns_of(head_of(spot, j * owned + i, owned))] for i in range(owned)],
            axis=1,
        )
        attn = local_ref[:, c] + dot(
            q_ref[:, c], diagonal([pieces[n][i] for i in range(owned)]), 1, 0
        )
        attn_ref[:, c] = attn
        guided = gain * u_ref[:, c].astype(F32)
        squares, crossed = attn * attn, guided * attn
        total_sq = sum(squares[:, head_columns(i)] for i in range(owned))
        total_cr = sum(crossed[:, head_columns(i)] for i in range(owned))
        sums = sums_ref if n else (before[1] if before else None)
        if sums is not None:
            total_sq = total_sq + sums[:rows]
            total_cr = total_cr + sums[rows:]
        sums_ref[:rows] = total_sq
        sums_ref[rows:] = total_cr
        for i in range(owned):
            far_ref[j * owned + i] = pieces[n][i]
        if j == final:
            total_sq = total_sq + pltpu.roll(total_sq, HD // 2, 1)
            total_cr = total_cr + pltpu.roll(total_cr, HD // 2, 1)
            fold_ref[...] = jnp.where(first_lanes(rows), total_sq, total_cr)


def grad_kernel(sums_count, features, group, spot, q_ref, attn_ref, u_ref, gain_ref, *refs):
    sums, g_ref, outs = refs[:sums_count], refs[sums_count], refs[sums_count + 1 :]
    rows = q_ref.shape[0]
    owned = outs[0].shape[0]
    total = sums[0][...]
    for other in sums[1:]:
        total = total + other[...]
    first = first_lanes(rows)
    square = jnp.sum(jnp.where(first, total, 0.0), axis=1, keepdims=True) / features
    cross = jnp.sum(jnp.where(first, 0.0, total), axis=1, keepdims=True) / features
    inverse = lax.rsqrt(square + 1e-06)
    a = jnp.broadcast_to(inverse, (rows, HD))
    b = jnp.broadcast_to(inverse * inverse * inverse * cross, (rows, HD))
    for n in range(group * owned):
        c = head_columns(n)
        gain = gain_ref[:, columns_of(head_of(spot, n, owned))]
        guided = gain * u_ref[:, c].astype(F32)
        grad = (a * guided - b * attn_ref[:, c]).astype(BF16)
        g_ref[:, c] = grad
        outs[n // owned][n % owned] = dot(q_ref[:, c], grad, 0, 0)


def query_kernel(step_heads, first, last, k_ref, v_ref, g_ref, state_ref, far_ref, *refs):
    scores_ref, gq_ref = refs[-2:]
    mask = causal()
    blocks = [pl.ds(b * CH, CH) for b in range(k_ref.shape[0] // CH)]

    def step(h, _):
        columns = step_columns(h, step_heads)
        for c in columns:
            for r in blocks:
                scores = jnp.where(mask, dot(g_ref[r, c], v_ref[r, c], 1, 1), 0.0)
                scores_ref[r, c] = scores.astype(BF16)
        for i, c in enumerate(columns):
            far = far_ref[h * step_heads + i]
            for r in blocks:
                before = (far + state_ref[r, c]).astype(BF16)
                gq = dot(scores_ref[r, c], k_ref[r, c], 1, 0) + dot(g_ref[r, c], before, 1, 1)
                gq_ref[r, c] = gq.astype(BF16)
        return 0

    lax.fori_loop(first, last, step, 0)


def near_kernel(step_heads, first, last, owned, spot, q_ref, k_ref, v_ref, g_ref, fwd_ref, back_ref, gq_ref, *refs):
    gk_ref, gv_ref, gq_out, states, sems = refs[-5:]
    lot = math.gcd(owned, step_heads)
    copies = []
    for n in range(first * step_heads // lot, last * step_heads // lot):
        there, here = lot_columns(spot, owned, lot, n)
        copies.append(pltpu.make_async_copy(gq_ref.at[:, here], gq_out.at[:, there], sems.at[n]))
    for copy in copies:
        copy.start()
    blocks = [pl.ds(b * CH, CH) for b in range(q_ref.shape[0] // CH)]

    def step(h, _):
        columns = step_columns(h, step_heads)
        for i, c in enumerate(columns):
            state = jnp.zeros((HD, HD), F32)
            for r in blocks[:0:-1]:
                state = state + dot(q_ref[r, c], g_ref[r, c], 0, 0)
                states[r, head_columns(i)] = state.astype(BF16)
        for i, c in enumerate(columns):
            for n, r in enumerate(blocks):
                gk = dot(back_ref[r, c], q_ref[r, c], 0, 0)
                gv = dot(fwd_ref[r, c], g_ref[r, c], 0, 0)
                if n + 1 < len(blocks):
                    near = states[blocks[n + 1], head_columns(i)]
                    gk = gk + dot(v_ref[r, c], near, 1, 1)
                    gv = gv + dot(k_ref[r, c], near, 1, 0)
                gk_ref[r, c] = gk
                gv_ref[r, c] = gv
        return 0

    lax.fori_loop(first, last, step, 0)
    for copy in copies:
        copy.wait()


def finish_kernel(slots, spot, k_ref, v_ref, gk_ref, gv_ref, *refs):
    pieces, (gk_out, gv_out, gk_buf, gv_buf, sems) = refs[: len(slots)], refs[-5:]
    owned = pieces[0].shape[0]
    copies = []
    for n, j in enumerate(slots):
        c = slice(j * owned * HD, (j + 1) * owned * HD)
        out = pl.ds(pl.multiple_of((spot[0] ^ j) * owned * HD, owned * HD), owned * HD)
        wide = diagonal([pieces[n][i] for i in range(owned)])
        gk_buf[n] = (gk_ref[:, c] + dot(v_ref[:, c], wide, 1, 1)).astype(BF16)
        copies.append(pltpu.make_async_copy(gk_buf.at[n], gk_out.at[:, out], sems.at[0, n]))
        copies[-1].start()
        gv_buf[n] = (gv_ref[:, c] + dot(k_ref[:, c], wide, 1, 0)).astype(BF16)
        copies.append(pltpu.make_async_copy(gv_buf.at[n], gv_out.at[:, out], sems.at[1, n]))
        copies[-1].start()
    for copy in copies:
        copy.wait()


LOCAL = pl.BlockSpec(memory_space=pltpu.VMEM)
SCALAR = pl.BlockSpec(memory_space=pltpu.SMEM)
FAR = pl.BlockSpec(memory_space=pltpu.HBM)


def call(kernel, args, in_specs, out_shape, out_specs, scratch=(), flops=0, aliases=None):
    moved = sum(a.size * a.dtype.itemsize for a in args)
    return pl.pallas_call(
        kernel,
        out_shape=out_shape,
        in_specs=in_specs,
        out_specs=out_specs,
        scratch_shapes=list(scratch),
        input_output_aliases=aliases or {},
        cost_estimate=pl.CostEstimate(flops=flops, bytes_accessed=moved, transcendentals=0),
        compiler_params=pltpu.CompilerParams(vmem_limit_bytes=VMEM_LIMIT),
    )(*args)


def on_device(query_act, key_act, value_act, upstream, norm_gain):
    peers, sides = lax.axis_size("seq"), lax.axis_size("head")
    rows, columns = query_act.shape
    heads = columns // HD
    group = group_size(peers, heads)
    owned = heads // group
    width = owned * HD
    spot = jnp.reshape(lax.axis_index("seq") % group, (1,)).astype(jnp.int32)
    gain = norm_gain.reshape(1, columns)
    shape = jax.ShapeDtypeStruct
    piece = shape((owned, HD, HD), F32)
    wide = shape((rows, columns), F32)
    half = shape((rows, columns), BF16)
    unit = 2 * rows * HD * HD * heads
    step_heads = next(n for n in (4, 2, 1) if heads % n == 0)
    steps = heads // step_heads

    def pieces_of(count, kernel, args, in_specs, out_shape, out_specs, scratch, flops, *more_static):
        outs = None
        count = min(count, steps)
        for n in range(count):
            first, last = n * steps // count, (n + 1) * steps // count
            more = [] if outs is None else list(outs)
            outs = call(
                functools.partial(kernel, step_heads, first, last, *more_static),
                [*args, *more], [*in_specs, *out_specs[: len(more)]], out_shape, out_specs,
                scratch, flops // count, {len(args) + i: i for i in range(len(more))},
            )
        return outs

    def exchange(parts):
        out = [parts[0]] + [None] * (group - 1)
        order = [j for j in SENDS if j < group]
        for j in order:
            out[j] = lax.ppermute(parts[j], "seq", [(s, s ^ j) for s in range(peers)])
        return out

    def moved(part, by, reverse):
        pairs = [(s, s + by) for s in range(peers - by)]
        return lax.ppermute(part, "seq", [(b, a) for a, b in pairs] if reverse else pairs)

    def exclusive(parts, reverse):
        got = exchange(parts)
        groups = peers // group
        carry = jnp.zeros_like(got[0])
        if groups > 1:
            total = call(
                functools.partial(total_kernel, group), got, [LOCAL] * group, piece, LOCAL
            )
            carry = moved(total, group, reverse)
            step = 1
            while step < groups - 1:
                carry = carry + moved(carry, group * step, reverse)
                step *= 2
        back = call(
            functools.partial(owner_kernel, reverse, group),
            [spot, carry, *got], [SCALAR] + [LOCAL] * (1 + group),
            [piece] * group, [LOCAL] * group,
        )
        return exchange(back)

    slots = [j for j in (0, *SENDS) if j < group]
    parts_of = [slots[a:b] for a, b in zip((0, *PARTS), (*PARTS, group)) if slots[a:b]]

    def by_arrival(kernel, args, in_specs, out_shape, out_specs, scratch, flops):
        outs = None
        for some in parts_of:
            more = [] if outs is None else list(outs)
            at = len(args) + len(some)
            outs = call(
                functools.partial(kernel, some),
                [*args, *(pieces[j] for j in some), *more],
                [*in_specs, *[LOCAL] * len(some), *out_specs[: len(more)]],
                out_shape, out_specs, scratch, flops * len(some) // group,
                {at + i: i for i in range(len(more))},
            )
        return outs

    key_near, value_near, *totals = call(
        functools.partial(kv_kernel, group, owned),
        [spot, in_hbm(key_act), in_hbm(value_act)], [SCALAR, FAR, FAR], [half, half] + [piece] * group,
        [LOCAL] * (2 + group), [pltpu.SemaphoreType.DMA((2, heads))], flops=unit,
    )
    local, scores, states, query_near, up_near = pieces_of(
        1, local_kernel,
        [spot, in_hbm(query_act), in_hbm(upstream), key_near, value_near],
        [SCALAR, FAR, FAR] + [LOCAL] * 2, [wide, half, wide, half, half], [LOCAL] * 5,
        [pltpu.SemaphoreType.DMA((2, heads))], 3 * unit, owned,
    )
    pieces = exclusive(totals, False)
    attn, _, far, sums = by_arrival(
        functools.partial(norm_kernel, slots[-1]), [spot, query_near, local, up_near, gain], [SCALAR] + [LOCAL] * 4,
        [wide, shape((2 * rows, HD), F32), shape((heads, HD, HD), F32),
         shape((rows, HD), F32)], [LOCAL] * 4, (), unit,
    )
    every = [sums] + [
        lax.ppermute(sums, "head", [(s, (s + t) % sides) for s in range(sides)])
        for t in range(1, sides)
    ]
    grad, *totals = call(
        functools.partial(grad_kernel, sides, float(columns * sides), group),
        [spot, query_near, attn, up_near, gain, *every], [SCALAR] + [LOCAL] * (4 + sides),
        [half] + [piece] * group, [LOCAL] * (1 + group), flops=unit,
    )
    back, near_q = pieces_of(
        1, query_kernel, [key_near, value_near, grad, states, far], [LOCAL] * 5,
        [half, half], [LOCAL] * 2, (), 3 * unit,
    )
    near_k, near_v, grad_q = pieces_of(
        1, near_kernel,
        [spot, query_near, key_near, value_near, grad, scores, back, near_q],
        [SCALAR] + [LOCAL] * 7, [wide, wide, half], [LOCAL, LOCAL, FAR],
        [pltpu.VMEM((rows, step_heads * HD), BF16), pltpu.SemaphoreType.DMA((heads,))],
        5 * unit, owned,
    )
    pieces = exclusive(totals, True)
    most = max(len(p) for p in parts_of)
    grad_k, grad_v = by_arrival(
        finish_kernel, [spot, key_near, value_near, near_k, near_v],
        [SCALAR] + [LOCAL] * 4, [half] * 2, [FAR] * 2,
        [pltpu.VMEM((most, rows, width), BF16)] * 2 + [pltpu.SemaphoreType.DMA((2, most))],
        2 * unit,
    )
    return grad_q, grad_k, grad_v


def solution(mesh):
    spec = P("seq", "head")

    return jax.shard_map(
        on_device, mesh=mesh, in_specs=(spec,) * 4 + (P("head"),), out_specs=(spec,) * 3,
        check_vma=False,
    )
```

```python
import functools
import math

import jax
import jax.numpy as jnp
from jax import lax
from jax.experimental import pallas as pl
from jax.experimental.pallas import tpu as pltpu
from jax.sharding import PartitionSpec as P


HD = 128
CH = 128
F32 = jnp.float32
BF16 = jnp.bfloat16
VMEM_LIMIT = 16 << 20
SENDS = (5, 2, 6, 1, 4, 3, 7)
PARTS = (7,)


def group_size(peers, heads):
    size = 1
    while size < 8 and peers % (2 * size) == 0 and heads % (2 * size) == 0:
        size *= 2
    return size


def dot(a, b, a_dim, b_dim):
    return lax.dot_general(a, b, (((a_dim,), (b_dim,)), ((), ())), preferred_element_type=F32)


def head_columns(i):
    return slice(i * HD, (i + 1) * HD)


def causal():
    rows = lax.broadcasted_iota(jnp.int32, (CH, CH), 0)
    columns = lax.broadcasted_iota(jnp.int32, (CH, CH), 1)
    return columns <= rows


def diagonal(blocks):
    if len(blocks) == 1:
        return blocks[0].astype(BF16)
    zero = jnp.zeros((HD, HD), BF16)
    lines = [
        jnp.concatenate([b.astype(BF16) if i == n else zero for n in range(len(blocks))], axis=1)
        for i, b in enumerate(blocks)
    ]
    return jnp.concatenate(lines, axis=0)


def in_hbm(x):
    return pltpu.with_memory_space_constraint(x, pltpu.HBM)


def step_columns(h, step_heads):
    first = h * step_heads * HD
    return [pl.ds(pl.multiple_of(first + i * HD, HD), HD) for i in range(step_heads)]


def head_of(spot, n, owned):
    return (spot[0] ^ (n // owned)) * owned + n % owned


def columns_of(head, count=1):
    return pl.ds(pl.multiple_of(head * HD, count * HD), count * HD)


def lot_columns(spot, owned, lot, n):
    return columns_of(head_of(spot, n * lot, owned), lot), columns_of(n * lot, lot)


def fetch(spot, owned, lot, n, far, near, sem):
    there, here = lot_columns(spot, owned, lot, n)
    return pltpu.make_async_copy(far.at[:, there], near.at[:, here], sem)


def kv_kernel(group, owned, spot, k_hbm, v_hbm, k_ref, v_ref, *refs):
    outs, sems = refs[:group], refs[group]
    copies = []
    for j in range(group):
        copies.append(
            [
                fetch(spot, owned, owned, j, k_hbm, k_ref, sems.at[0, j]),
                fetch(spot, owned, owned, j, v_hbm, v_ref, sems.at[1, j]),
            ]
        )
        for copy in copies[-1]:
            copy.start()
    for n in range(group * owned):
        if n % owned == 0:
            for copy in copies[n // owned]:
                copy.wait()
        c = head_columns(n)
        outs[n // owned][n % owned] = dot(k_ref[:, c], v_ref[:, c], 0, 0)


def local_kernel(step_heads, first, last, owned, spot, q_hbm, u_hbm, k_ref, v_ref, *refs):
    attn_ref, scores_ref, state_ref, q_ref, u_ref, turned_ref, sems = refs[-7:]
    mask = causal()

    lot = math.gcd(owned, step_heads)
    lots = step_heads // lot

    def get_q(n):
        return fetch(spot, owned, lot, n, q_hbm, q_ref, sems.at[0, n])

    def get_u(n):
        return fetch(spot, owned, lot, n, u_hbm, u_ref, sems.at[1, n])

    mine = range(first * lots, last * lots)
    for get in (get_q, get_u):
        for n in mine:
            get(n).start()
    blocks = [pl.ds(b * CH, CH) for b in range(q_ref.shape[0] // CH)]

    def step(h, _):
        columns = step_columns(h, step_heads)
        for c in columns:
            state = jnp.zeros((HD, HD), F32)
            for r in blocks:
                state_ref[r, c] = state
                if r is not blocks[-1]:
                    state = state + dot(k_ref[r, c], v_ref[r, c], 0, 0)
        for i in range(lots):
            get_q(h * lots + i).wait()
        for c in columns:
            for r in blocks:
                turned_ref[c, r] = q_ref[r, c].T
                scores = jnp.where(mask, dot(q_ref[r, c], k_ref[r, c], 1, 1), 0.0)
                scores_ref[r, c] = scores.astype(BF16)
        for c in columns:
            for r in blocks:
                attn = dot(scores_ref[r, c], v_ref[r, c], 1, 0)
                if r is not blocks[0]:
                    attn = attn + dot(q_ref[r, c], state_ref[r, c].astype(BF16), 1, 0)
                attn_ref[r, c] = attn
        return 0

    lax.fori_loop(first, last, step, 0)
    for n in mine:
        get_u(n).wait()


def total_kernel(count, *refs):
    total = refs[0][...]
    for ref in refs[1:count]:
        total = total + ref[...]
    refs[count][...] = total


def owner_kernel(reverse, count, spot, carry, *refs):
    got, outs = refs[:count], refs[count:]
    me = spot[0]
    for n in range(count):
        part = carry[...]
        for m in range(count):
            inside = (me ^ m) > (me ^ n) if reverse else (me ^ m) < (me ^ n)
            if m != n:
                part = part + jnp.where(inside, got[m][...], 0.0)
        outs[n][...] = part


def first_lanes(rows):
    return lax.broadcasted_iota(jnp.int32, (rows, HD), 1) < HD // 2


def norm_kernel(final, slots, spot, q_ref, local_ref, u_ref, gain_ref, *refs):
    pieces, before = refs[: len(slots)], refs[len(slots) : -4]
    attn_ref, sums_ref, far_ref, fold_ref = refs[-4:]
    rows = q_ref.shape[0]
    owned = pieces[0].shape[0]
    for n, j in enumerate(slots):
        c = slice(j * owned * HD, (j + 1) * owned * HD)
        gain = jnp.concatenate(
            [gain_ref[:, columns_of(head_of(spot, j * owned + i, owned))] for i in range(owned)],
            axis=1,
        )
        attn = local_ref[:, c] + dot(
            q_ref[:, c], diagonal([pieces[n][i] for i in range(owned)]), 1, 0
        )
        attn_ref[:, c] = attn
        guided = gain * u_ref[:, c].astype(F32)
        squares, crossed = attn * attn, guided * attn
        total_sq = sum(squares[:, head_columns(i)] for i in range(owned))
        total_cr = sum(crossed[:, head_columns(i)] for i in range(owned))
        sums = sums_ref if n else (before[1] if before else None)
        if sums is not None:
            total_sq = total_sq + sums[:rows]
            total_cr = total_cr + sums[rows:]
        sums_ref[:rows] = total_sq
        sums_ref[rows:] = total_cr
        for i in range(owned):
            far_ref[j * owned + i] = pieces[n][i]
        if j == final:
            total_sq = total_sq + pltpu.roll(total_sq, HD // 2, 1)
            total_cr = total_cr + pltpu.roll(total_cr, HD // 2, 1)
            fold_ref[...] = jnp.where(first_lanes(rows), total_sq, total_cr)


def grad_kernel(sums_count, features, group, spot, q_ref, attn_ref, u_ref, gain_ref, *refs):
    sums, g_ref, outs = refs[:sums_count], refs[sums_count], refs[sums_count + 1 :]
    rows = q_ref.shape[1]
    owned = outs[0].shape[0]
    total = sums[0][...]
    for other in sums[1:]:
        total = total + other[...]
    first = first_lanes(rows)
    square = jnp.sum(jnp.where(first, total, 0.0), axis=1, keepdims=True) / features
    cross = jnp.sum(jnp.where(first, 0.0, total), axis=1, keepdims=True) / features
    inverse = lax.rsqrt(square + 1e-06)
    a = jnp.broadcast_to(inverse, (rows, HD))
    b = jnp.broadcast_to(inverse * inverse * inverse * cross, (rows, HD))
    for n in range(group * owned):
        c = head_columns(n)
        gain = gain_ref[:, columns_of(head_of(spot, n, owned))]
        guided = gain * u_ref[:, c].astype(F32)
        grad = (a * guided - b * attn_ref[:, c]).astype(BF16)
        g_ref[:, c] = grad
        outs[n // owned][n % owned] = dot(q_ref[c, :], grad, 1, 0)


def query_kernel(step_heads, first, last, k_ref, v_ref, g_ref, state_ref, far_ref, *refs):
    scores_ref, gq_ref = refs[-2:]
    mask = causal()
    blocks = [pl.ds(b * CH, CH) for b in range(k_ref.shape[0] // CH)]

    def step(h, _):
        columns = step_columns(h, step_heads)
        for c in columns:
            for r in blocks:
                scores = jnp.where(mask, dot(g_ref[r, c], v_ref[r, c], 1, 1), 0.0)
                scores_ref[r, c] = scores.astype(BF16)
        for i, c in enumerate(columns):
            far = far_ref[h * step_heads + i]
            for r in blocks:
                before = (far + state_ref[r, c]).astype(BF16)
                gq = dot(scores_ref[r, c], k_ref[r, c], 1, 0) + dot(g_ref[r, c], before, 1, 1)
                gq_ref[r, c] = gq.astype(BF16)
        return 0

    lax.fori_loop(first, last, step, 0)


def near_kernel(step_heads, first, last, owned, spot, q_ref, k_ref, v_ref, g_ref, fwd_ref, back_ref, gq_ref, *refs):
    gk_ref, gv_ref, gq_out, states, sems = refs[-5:]
    lot = math.gcd(owned, step_heads)
    copies = []
    for n in range(first * step_heads // lot, last * step_heads // lot):
        there, here = lot_columns(spot, owned, lot, n)
        copies.append(pltpu.make_async_copy(gq_ref.at[:, here], gq_out.at[:, there], sems.at[n]))
    for copy in copies:
        copy.start()
    blocks = [pl.ds(b * CH, CH) for b in range(q_ref.shape[0] // CH)]

    def step(h, _):
        columns = step_columns(h, step_heads)
        for i, c in enumerate(columns):
            state = jnp.zeros((HD, HD), F32)
            for r in blocks[:0:-1]:
                state = state + dot(q_ref[r, c], g_ref[r, c], 0, 0)
                states[r, head_columns(i)] = state.astype(BF16)
        for i, c in enumerate(columns):
            for n, r in enumerate(blocks):
                gk = dot(back_ref[r, c], q_ref[r, c], 0, 0)
                gv = dot(fwd_ref[r, c], g_ref[r, c], 0, 0)
                if n + 1 < len(blocks):
                    near = states[blocks[n + 1], head_columns(i)]
                    gk = gk + dot(v_ref[r, c], near, 1, 1)
                    gv = gv + dot(k_ref[r, c], near, 1, 0)
                gk_ref[r, c] = gk
                gv_ref[r, c] = gv
        return 0

    lax.fori_loop(first, last, step, 0)
    for copy in copies:
        copy.wait()


def finish_kernel(slots, spot, k_ref, v_ref, gk_ref, gv_ref, *refs):
    pieces, (gk_out, gv_out, gk_buf, gv_buf, sems) = refs[: len(slots)], refs[-5:]
    owned = pieces[0].shape[0]
    copies = []
    for n, j in enumerate(slots):
        c = slice(j * owned * HD, (j + 1) * owned * HD)
        out = pl.ds(pl.multiple_of((spot[0] ^ j) * owned * HD, owned * HD), owned * HD)
        wide = diagonal([pieces[n][i] for i in range(owned)])
        gk_buf[n] = (gk_ref[:, c] + dot(v_ref[:, c], wide, 1, 1)).astype(BF16)
        copies.append(pltpu.make_async_copy(gk_buf.at[n], gk_out.at[:, out], sems.at[0, n]))
        copies[-1].start()
        gv_buf[n] = (gv_ref[:, c] + dot(k_ref[:, c], wide, 1, 0)).astype(BF16)
        copies.append(pltpu.make_async_copy(gv_buf.at[n], gv_out.at[:, out], sems.at[1, n]))
        copies[-1].start()
    for copy in copies:
        copy.wait()


LOCAL = pl.BlockSpec(memory_space=pltpu.VMEM)
SCALAR = pl.BlockSpec(memory_space=pltpu.SMEM)
FAR = pl.BlockSpec(memory_space=pltpu.HBM)


def call(kernel, args, in_specs, out_shape, out_specs, scratch=(), flops=0, aliases=None):
    moved = sum(a.size * a.dtype.itemsize for a in args)
    return pl.pallas_call(
        kernel,
        out_shape=out_shape,
        in_specs=in_specs,
        out_specs=out_specs,
        scratch_shapes=list(scratch),
        input_output_aliases=aliases or {},
        cost_estimate=pl.CostEstimate(flops=flops, bytes_accessed=moved, transcendentals=0),
        compiler_params=pltpu.CompilerParams(vmem_limit_bytes=VMEM_LIMIT),
    )(*args)


def on_device(query_act, key_act, value_act, upstream, norm_gain):
    peers, sides = lax.axis_size("seq"), lax.axis_size("head")
    rows, columns = query_act.shape
    heads = columns // HD
    group = group_size(peers, heads)
    owned = heads // group
    width = owned * HD
    spot = jnp.reshape(lax.axis_index("seq") % group, (1,)).astype(jnp.int32)
    gain = norm_gain.reshape(1, columns)
    shape = jax.ShapeDtypeStruct
    piece = shape((owned, HD, HD), F32)
    wide = shape((rows, columns), F32)
    half = shape((rows, columns), BF16)
    unit = 2 * rows * HD * HD * heads
    step_heads = next(n for n in (4, 2, 1) if heads % n == 0)
    steps = heads // step_heads

    def pieces_of(count, kernel, args, in_specs, out_shape, out_specs, scratch, flops, *more_static):
        outs = None
        count = min(count, steps)
        for n in range(count):
            first, last = n * steps // count, (n + 1) * steps // count
            more = [] if outs is None else list(outs)
            outs = call(
                functools.partial(kernel, step_heads, first, last, *more_static),
                [*args, *more], [*in_specs, *out_specs[: len(more)]], out_shape, out_specs,
                scratch, flops // count, {len(args) + i: i for i in range(len(more))},
            )
        return outs

    def exchange(parts):
        out = [parts[0]] + [None] * (group - 1)
        order = [j for j in SENDS if j < group]
        for j in order:
            out[j] = lax.ppermute(parts[j], "seq", [(s, s ^ j) for s in range(peers)])
        return out

    def moved(part, by, reverse):
        pairs = [(s, s + by) for s in range(peers - by)]
        return lax.ppermute(part, "seq", [(b, a) for a, b in pairs] if reverse else pairs)

    def exclusive(parts, reverse):
        got = exchange(parts)
        groups = peers // group
        carry = jnp.zeros_like(got[0])
        if groups > 1:
            total = call(
                functools.partial(total_kernel, group), got, [LOCAL] * group, piece, LOCAL
            )
            carry = moved(total, group, reverse)
            step = 1
            while step < groups - 1:
                carry = carry + moved(carry, group * step, reverse)
                step *= 2
        back = call(
            functools.partial(owner_kernel, reverse, group),
            [spot, carry, *got], [SCALAR] + [LOCAL] * (1 + group),
            [piece] * group, [LOCAL] * group,
        )
        return exchange(back)

    slots = [j for j in (0, *SENDS) if j < group]
    parts_of = [slots[a:b] for a, b in zip((0, *PARTS), (*PARTS, group)) if slots[a:b]]

    def by_arrival(kernel, args, in_specs, out_shape, out_specs, scratch, flops):
        outs = None
        for some in parts_of:
            more = [] if outs is None else list(outs)
            at = len(args) + len(some)
            outs = call(
                functools.partial(kernel, some),
                [*args, *(pieces[j] for j in some), *more],
                [*in_specs, *[LOCAL] * len(some), *out_specs[: len(more)]],
                out_shape, out_specs, scratch, flops * len(some) // group,
                {at + i: i for i in range(len(more))},
            )
        return outs

    key_near, value_near, *totals = call(
        functools.partial(kv_kernel, group, owned),
        [spot, in_hbm(key_act), in_hbm(value_act)], [SCALAR, FAR, FAR], [half, half] + [piece] * group,
        [LOCAL] * (2 + group), [pltpu.SemaphoreType.DMA((2, heads))], flops=unit,
    )
    local, scores, states, query_near, up_near, turned = pieces_of(
        1, local_kernel,
        [spot, in_hbm(query_act), in_hbm(upstream), key_near, value_near],
        [SCALAR, FAR, FAR] + [LOCAL] * 2, [wide, half, wide, half, half, shape((columns, rows), BF16)],
        [LOCAL] * 6,
        [pltpu.SemaphoreType.DMA((2, heads))], 3 * unit, owned,
    )
    pieces = exclusive(totals, False)
    attn, _, far, sums = by_arrival(
        functools.partial(norm_kernel, slots[-1]), [spot, query_near, local, up_near, gain], [SCALAR] + [LOCAL] * 4,
        [wide, shape((2 * rows, HD), F32), shape((heads, HD, HD), F32),
         shape((rows, HD), F32)], [LOCAL] * 4, (), unit,
    )
    every = [sums] + [
        lax.ppermute(sums, "head", [(s, (s + t) % sides) for s in range(sides)])
        for t in range(1, sides)
    ]
    grad, *totals = call(
        functools.partial(grad_kernel, sides, float(columns * sides), group),
        [spot, turned, attn, up_near, gain, *every], [SCALAR] + [LOCAL] * (4 + sides),
        [half] + [piece] * group, [LOCAL] * (1 + group), flops=unit,
    )
    back, near_q = pieces_of(
        1, query_kernel, [key_near, value_near, grad, states, far], [LOCAL] * 5,
        [half, half], [LOCAL] * 2, (), 3 * unit,
    )
    near_k, near_v, grad_q = pieces_of(
        1, near_kernel,
        [spot, query_near, key_near, value_near, grad, scores, back, near_q],
        [SCALAR] + [LOCAL] * 7, [wide, wide, half], [LOCAL, LOCAL, FAR],
        [pltpu.VMEM((rows, step_heads * HD), BF16), pltpu.SemaphoreType.DMA((heads,))],
        5 * unit, owned,
    )
    pieces = exclusive(totals, True)
    most = max(len(p) for p in parts_of)
    grad_k, grad_v = by_arrival(
        finish_kernel, [spot, key_near, value_near, near_k, near_v],
        [SCALAR] + [LOCAL] * 4, [half] * 2, [FAR] * 2,
        [pltpu.VMEM((most, rows, width), BF16)] * 2 + [pltpu.SemaphoreType.DMA((2, most))],
        2 * unit,
    )
    return grad_q, grad_k, grad_v


def solution(mesh):
    spec = P("seq", "head")

    return jax.shard_map(
        on_device, mesh=mesh, in_specs=(spec,) * 4 + (P("head"),), out_specs=(spec,) * 3,
        check_vma=False,
    )
```
